32 devices in a mesh: pipe: 2 (over y), expert: 16 (over z, x, core).
Axes of the slice: x: 2, y: 2, z: 4, core: 2. Of those that a mesh axis runs over, the one named last changes fastest.
Arguments:
- bwd_input: bfloat16 [2, 2048, 2048], P('pipe', 'expert'), may hold values from -6 to 6
- out_grad: bfloat16 [2, 2048, 2048], P('pipe', 'expert'), may hold values from -6 to 6
- norm_gain: float32 [2, 2048], P('pipe'), may hold values from 0.1 to 1.9
- up_weight: bfloat16 [2, 16, 2048, 768], P('pipe', 'expert'), may hold values from -0.125 to 0.125
- down_weight: bfloat16 [2, 16, 768, 2048], P('pipe', 'expert'), may hold values from -0.21875 to 0.21875
- bwd_routes: int32 [2, 2048, 8], P('pipe', 'expert'), may hold values from 0 to 15, all different within a row; in each aligned block of 128 rows (0 to 127, 128 to 255, ..., all dimensions but the last counted through in order) at most 80 rows name the same one
- bwd_gates: bfloat16 [2, 2048, 8], P('pipe', 'expert'), may hold values from 0.19921875 to 1
Outputs:
- prev_grad: bfloat16 [2, 2048, 2048], P('pipe', 'expert')
The draws below stay inside these ranges and needn't reach their ends.
Inputs may be any that keep to these rules, and one draw needn't show every extreme that they name: `bwd_routes`: A token's 8 routes name different experts. Among the 128 tokens of one index of expert (aligned blocks of rows, sections taken in order) at most 80 name any one expert, and in every draw some expert is named by exactly 80 tokens of some block.
All inputs are finite; a program needn't handle non-finite values.
Results may differ from the reference program's by a relative error of at most 0.0053.
Values may be sent and summed in bfloat16 or wider, within the bound.
No kernel may reach another device: no remote copies, remote signals or barrier semaphores. Data moves between devices by JAX's collectives and lax.ppermute only.
A program may use at most 128 MiB of HBM per device.

```python
import math
import jax
import jax.numpy as jnp
import numpy as np
from jax import lax

D = 2048
FF = 768
TOP = 8
TOK_DEV = 128
SECTIONS = 2
EXPERTS = 16
TOKENS = 2048
CAP = 80


def level_of(key, dims, pieces, least, high):
    level = 1.0
    for dim, shards_of in pieces:
        heights = jax.random.uniform(jax.random.fold_in(jax.random.fold_in(key, 6), dim), (shards_of,), jnp.float32, least / len(pieces), high / len(pieces))
        level = level * jnp.repeat(jnp.exp(heights), dims[dim] // shards_of).reshape((-1,) + (1,) * (len(dims) - 1 - dim))
    return level


def assign_block(stream_key, own, number, rows, count, top, bound, slope):
    ranking = jax.random.permutation(stream_key, count)
    packed, usual = shares(count, rows * top, bound, slope, True), shares(count, rows * top, bound, slope, False)
    places = jnp.arange(count)

    def named(sizes, turn):
        used = int((sizes > 0).sum())
        fixed = max(1, used // 4)
        passed = fixed + (places - fixed + turn * (used - fixed)) % max(1, count - fixed)
        return jnp.zeros((count,), jnp.int32).at[ranking[jnp.where(places < fixed, places, passed)]].set(jnp.asarray(sizes, jnp.int32))

    sizes = jnp.where(number % 4 == 0, named(packed, number // 4), named(usual, number - number // 4 - 1))
    mixed = jax.random.permutation(jax.random.fold_in(own, 3), count)
    source_of, taker = mixed[0:count // 2 * 2:2], mixed[1:count // 2 * 2:2]
    slack = jnp.minimum(sizes[source_of] - 1, bound - sizes[taker]) // 2
    slack = jnp.where((source_of == ranking[0]) | (taker == ranking[0]) | (sizes[taker] == 0), 0, jnp.maximum(slack, 0))
    passed = jax.random.randint(jax.random.fold_in(own, 4), (count // 2,), 0, 1 << 20) % (slack + 1)
    sizes = sizes.at[source_of].add(-passed).at[taker].add(passed)
    items = jnp.searchsorted(jnp.cumsum(sizes), jnp.arange(rows * top), side="right").astype(jnp.int32)
    listing = items.reshape(top, rows).T
    listing = listing[jax.random.permutation(jax.random.fold_in(own, 1), rows)]
    turn = jax.random.randint(jax.random.fold_in(own, 2), (rows, 1), 0, top)
    return jnp.take_along_axis(listing, (jnp.arange(top)[None, :] + turn) % top, axis=1)


def shares(number_of, total, bound, lean, full):
    portions = [(1 << 20) // math.isqrt(standing ** lean) + 1 for standing in range(1, number_of + 1)]
    largest = bound if full else min(bound, max(-(-total // number_of), total * portions[0] // sum(portions)))
    least = 1 if total - largest >= number_of - 1 else 0
    given, rest = [largest] + [least] * (number_of - 1), total - largest - least * (number_of - 1)
    while rest > 0:
        free = [i for i in range(1, number_of) if given[i] < largest] or [i for i in range(1, number_of) if given[i] < bound]
        whole, budget = sum([portions[i] for i in free]), rest
        for i in free:
            more = min(bound - given[i], max(1, budget * portions[i] // whole), rest)
            given[i] = given[i] + more
            rest = rest - more
    return np.array(given)


def gaussian(rng, shape, spread, reach, shards=(), kind=jnp.bfloat16):
    values = jax.random.normal(rng, shape, jnp.float32) * spread
    if len(shards) > 0:
        values = level_of(rng, shape, shards, -0.22, 0.18) * values
    return jnp.clip(values, min=-reach, max=reach).astype(kind)


def setup_inputs(seed: int = 0) -> dict:
    keys = jax.random.split(jax.random.key(seed), 8)
    bwd_input = gaussian(keys[0], (SECTIONS, TOKENS, D), 1.0, 6.0, ((0, 2), (1, 16)))
    out_grad = gaussian(keys[1], (SECTIONS, TOKENS, D), 1.0, 6.0, ((0, 2), (1, 16)))
    norm_gain = jnp.clip(1.0 + 0.18 * jax.random.normal(keys[2], (SECTIONS, D), jnp.float32), 0.1, 1.9)
    up_weight = gaussian(keys[3], (SECTIONS, EXPERTS, D, FF), D ** -0.5, 0.125, ((0, 2), (1, 16)))
    down_weight = gaussian(keys[4], (SECTIONS, EXPERTS, FF, D), FF ** -0.5, 0.21875, ((0, 2), (1, 16)))
    bwd_routes_keys = jax.random.split(jax.random.fold_in(keys[5], 1), SECTIONS * TOKENS // TOK_DEV)
    bwd_routes_turns = jax.random.permutation(jax.random.fold_in(keys[5], 3), SECTIONS * TOKENS // TOK_DEV)
    bwd_routes = jax.vmap(lambda own, number: assign_block(jax.random.fold_in(keys[5], 2), own, number, TOK_DEV, EXPERTS, TOP, CAP, 2))(bwd_routes_keys, bwd_routes_turns).reshape((SECTIONS, TOKENS, TOP))
    bwd_gates = jnp.clip(jnp.exp(math.log(1.0) - 1.6133518 * jax.random.uniform(keys[6], (SECTIONS, TOKENS, TOP), jnp.float32) ** level_of(keys[6], (SECTIONS, TOKENS, TOP), ((0, 2), (1, 16)), -0.2, 0.2)), 0.19921875, 1.0).astype(jnp.bfloat16)
    return {"bwd_input": bwd_input, "out_grad": out_grad, "norm_gain": norm_gain, "up_weight": up_weight, "down_weight": down_weight, "bwd_routes": bwd_routes, "bwd_gates": bwd_gates}


epsilon = 1e-06

def normalize(inputs, gain_row):
    values = inputs.astype(jnp.float32)
    scaling = lax.rsqrt(lax.optimization_barrier(jnp.mean(values * values, axis=-1, keepdims=True)) + epsilon)
    return ((values * scaling * gain_row[None, :]).astype(jnp.bfloat16), values, scaling)

def norm_back(values, scaling, gain_row, d_normed):
    weighted = gain_row[None, :] * d_normed
    inner_mean = lax.optimization_barrier(jnp.mean(values * weighted, axis=-1, keepdims=True))
    return scaling * weighted - values * (scaling * scaling * scaling) * inner_mean

def expert_backward(row_block, grad_block, up_matrix, down_matrix):
    before = jnp.dot(row_block, up_matrix, preferred_element_type=jnp.float32)
    d_hidden = jnp.dot(grad_block, down_matrix.T, preferred_element_type=jnp.float32)
    sigmoid_of = jax.nn.sigmoid(before)
    d_before = (d_hidden * sigmoid_of * (1.0 + before * (1.0 - sigmoid_of))).astype(jnp.bfloat16)
    return jnp.dot(d_before, up_matrix.T, preferred_element_type=jnp.float32).astype(jnp.bfloat16)

def slot_index(routes):
    chosen = routes[:, :, None] == jnp.arange(EXPERTS, dtype=jnp.int32)[None, None, :]
    member = lax.optimization_barrier(jnp.sum(chosen.astype(jnp.int32), axis=1)).astype(jnp.int32)
    blocks = member.reshape(TOKENS // TOK_DEV, TOK_DEV, EXPERTS)
    rank_in = (jnp.cumsum(blocks, axis=1) - blocks).astype(jnp.int32).reshape(TOKENS, EXPERTS)
    slot_of = lax.optimization_barrier(jnp.sum(jnp.where(chosen, rank_in[:, None, :], 0), axis=2)).astype(jnp.int32)
    source = (jnp.arange(TOKENS, dtype=jnp.int32) // TOK_DEV)[:, None]
    per_expert = TOKENS // TOK_DEV * CAP
    position = (source * CAP + slot_of).astype(jnp.int32)
    owners = jnp.broadcast_to(jnp.arange(TOKENS, dtype=jnp.int32)[:, None], routes.shape).astype(jnp.int32)
    table = jnp.full((EXPERTS, per_expert), TOKENS, jnp.int32).at[routes, position].set(owners)
    return (table, (routes * per_expert + position).astype(jnp.int32))

def one_section(x_bwd, grad_rows, gain_row, ups, downs, routes_b, gates_b):
    normed_b, values_b, scaling_b = normalize(x_bwd, gain_row)
    table_b, where_b = slot_index(routes_b)
    padded_b = jnp.concatenate([normed_b, jnp.zeros((1, D), normed_b.dtype)], axis=0)
    padded_g = jnp.concatenate([grad_rows, jnp.zeros((1, D), grad_rows.dtype)], axis=0)

    def backward_one(operands):
        table_row, up_matrix, down_matrix = operands
        return expert_backward(padded_b[table_row], padded_g[table_row], up_matrix, down_matrix)
    results_b = lax.map(backward_one, (table_b, ups, downs))
    picked_b = jnp.take(results_b.reshape(-1, D), where_b, axis=0)
    d_normed = lax.optimization_barrier(jnp.sum(gates_b.astype(jnp.float32)[:, :, None] * picked_b.astype(jnp.float32), axis=1))
    return (grad_rows.astype(jnp.float32) + norm_back(values_b, scaling_b, gain_row, d_normed)).astype(jnp.bfloat16)

def reference(bwd_input, out_grad, norm_gain, up_weight, down_weight, bwd_routes, bwd_gates):
    gradients = []
    for section in range(SECTIONS):
        gradients.append(one_section(bwd_input[section], out_grad[section], norm_gain[section], up_weight[section], down_weight[section], bwd_routes[section], bwd_gates[section]))
    return jnp.roll(jnp.stack(gradients), -1, axis=0)
```

```python
import jax
import jax.numpy as jnp
from jax import lax
from jax.experimental import pallas as pl
from jax.experimental.pallas import tpu as pltpu
from jax.sharding import PartitionSpec as P

epsilon = 1e-06
LANES = 128
NT = (((1,), (1,)), ((), ()))


def pack_kernel(x_ref, g_ref, gain_ref, routes_ref, gates_ref, up_ref, down_ref):
    half, width = up_ref.shape[0], x_ref.shape[1]
    values = x_ref[...].astype(jnp.float32)
    scaling = lax.rsqrt(jnp.mean(values * values, axis=-1, keepdims=True) + epsilon)
    normed = (values * scaling * gain_ref[...]).astype(jnp.bfloat16)
    lanes = up_ref.shape[1] - 2 * width
    lane = lax.broadcasted_iota(jnp.int32, (x_ref.shape[0], lanes), 1)
    dense = jnp.zeros((x_ref.shape[0], lanes), jnp.float32)
    routes, gates = routes_ref[...], gates_ref[...].astype(jnp.float32)
    for k in range(routes.shape[1]):
        dense = dense + jnp.where(lane == routes[:, k : k + 1], gates[:, k : k + 1], 0.0)
    dense = dense.astype(jnp.bfloat16)
    for ref, first in ((up_ref, 0), (down_ref, half)):
        ref[:, :width] = normed[first : first + half]
        ref[:, width : 2 * width] = g_ref[first : first + half, :]
        ref[:, 2 * width :] = dense[first : first + half]


def pack(x, grad, gain, routes, gates, experts):
    rows, width = x.shape
    lanes = -(-experts // LANES) * LANES
    shape = jax.ShapeDtypeStruct((rows // 2, 2 * width + lanes), jnp.bfloat16)
    return pl.pallas_call(
        pack_kernel,
        out_shape=(shape, shape),
        compiler_params=pltpu.CompilerParams(vmem_limit_bytes=40 << 20),
        name="pack",
    )(x, grad, gain, routes, gates)


def expert_kernel(me_ref, a_ref, b_ref, u0_ref, u1_ref, d0_ref, d1_ref, o_ref, n_s, g_s, w_s):
    width = u0_ref.shape[0]
    half = a_ref.shape[0]

    @pl.when(pl.program_id(0) == 0)
    def _():
        lane = lax.broadcasted_iota(jnp.int32, (half, a_ref.shape[1] - 2 * width), 1)
        for ref, first in ((a_ref, 0), (b_ref, half)):
            n_s[first : first + half, :] = ref[:, :width]
            g_s[first : first + half, :] = ref[:, width : 2 * width]
            dense = ref[:, 2 * width :].astype(jnp.float32)
            for i in range(2):
                w_s[first : first + half, i : i + 1] = jnp.sum(
                    jnp.where(lane == me_ref[i], dense, 0.0), axis=-1, keepdims=True
                )

    total = None
    for i, (u_ref, d_ref) in enumerate(((u0_ref, d0_ref), (u1_ref, d1_ref))):
        before = jnp.dot(n_s[...], u_ref[...], preferred_element_type=jnp.float32)
        d_hidden = lax.dot_general(g_s[...], d_ref[...], NT, preferred_element_type=jnp.float32)
        sigmoid_of = jax.nn.sigmoid(before)
        d_before = d_hidden * sigmoid_of * (1.0 + before * (1.0 - sigmoid_of))
        d_before = (d_before * w_s[:, i : i + 1]).astype(jnp.bfloat16)
        part = lax.dot_general(d_before, u_ref[...], NT, preferred_element_type=jnp.float32)
        total = part if total is None else total + part

    @pl.when(pl.program_id(0) == 0)
    def _():
        o_ref[...] = total

    @pl.when(pl.program_id(0) > 0)
    def _():
        o_ref[...] += total


def expert_part(me, a, b, u0, u1, d0, d1):
    half, wide = a.shape
    width, hidden = u0.shape
    chunk = 256
    up = pl.BlockSpec((width, chunk), lambda i: (0, i))
    down = pl.BlockSpec((chunk, width), lambda i: (i, 0))
    rows = pl.BlockSpec((half, wide), lambda i: (0, 0))
    return pl.pallas_call(
        expert_kernel,
        out_shape=jax.ShapeDtypeStruct((2 * half, width), jnp.float32),
        grid=(hidden // chunk,),
        in_specs=[pl.BlockSpec(memory_space=pltpu.SMEM), rows, rows, up, up, down, down],
        out_specs=pl.BlockSpec((2 * half, width), lambda i: (0, 0)),
        scratch_shapes=[
            pltpu.VMEM((2 * half, width), jnp.bfloat16),
            pltpu.VMEM((2 * half, width), jnp.bfloat16),
            pltpu.VMEM((2 * half, LANES), jnp.float32),
        ],
        compiler_params=pltpu.CompilerParams(
            dimension_semantics=("arbitrary",), vmem_limit_bytes=40 << 20
        ),
        cost_estimate=pl.CostEstimate(
            flops=24 * half * width * hidden,
            transcendentals=4 * half * hidden,
            bytes_accessed=8 * width * hidden + 12 * half * width,
        ),
        name="expert_part",
    )(me, a, b, u0, u1, d0, d1)


def finish_kernel(x_ref, g_ref, gain_ref, own_ref, a_ref, b_ref, o_ref):
    half = a_ref.shape[0]
    for ref, first in ((a_ref, 0), (b_ref, half)):
        part = slice(first, first + half)
        values = x_ref[part, :].astype(jnp.float32)
        scaling = lax.rsqrt(jnp.mean(values * values, axis=-1, keepdims=True) + epsilon)
        d_normed = own_ref[part, :].astype(jnp.float32) + ref[...].astype(jnp.float32)
        weighted = gain_ref[...] * d_normed
        inner_mean = jnp.mean(values * weighted, axis=-1, keepdims=True)
        back = scaling * weighted - values * (scaling * scaling * scaling) * inner_mean
        o_ref[part, :] = (g_ref[part, :].astype(jnp.float32) + back).astype(jnp.bfloat16)


def finish(x, grad, gain, own, a, b):
    return pl.pallas_call(
        finish_kernel,
        out_shape=jax.ShapeDtypeStruct(x.shape, jnp.bfloat16),
        compiler_params=pltpu.CompilerParams(vmem_limit_bytes=40 << 20),
        name="finish",
    )(x, grad, gain, own, a, b)


def shards(bwd_input, out_grad, norm_gain, up_weight, down_weight, bwd_routes, bwd_gates):
    experts = lax.axis_size("expert")
    sections = lax.axis_size("pipe")
    chips = experts // 2
    ring = list(range(0, chips, 2)) + list(range(1, chips, 2))[::-1]

    def hop(value, by):
        moves = [(ring[i], ring[(i + by) % chips]) for i in range(chips)]
        return lax.ppermute(value, "expert", [(2 * a + c, 2 * b + c) for a, b in moves for c in (0, 1)])

    def last_hop(value, by):
        moves = [(ring[i], ring[(i + by) % chips]) for i in range(chips)]
        return lax.ppermute(
            value,
            ("pipe", "expert"),
            [
                (s * experts + 2 * a + c, (s - 1) % sections * experts + 2 * b + c)
                for s in range(sections)
                for a, b in moves
                for c in (0, 1)
            ],
        )

    def to_previous(value):
        return lax.ppermute(value, "pipe", [(s, (s - 1) % sections) for s in range(sections)])

    def swap(value):
        return lax.ppermute(value, "expert", [(e, e ^ 1) for e in range(experts)])

    x, grad = bwd_input[0], out_grad[0]
    u0, d0 = up_weight[0, 0], down_weight[0, 0]
    e = lax.axis_index("expert").astype(jnp.int32)
    me = jnp.stack([e, e ^ 1])

    a, b = pack(x, grad, norm_gain, bwd_routes[0], bwd_gates[0], experts)
    a1, b1 = hop(a, 1), hop(b, -1)
    u1, d1 = swap(u0), swap(d0)
    x_out, grad_out, gain_out = to_previous(x), to_previous(grad), to_previous(norm_gain)
    own = to_previous(expert_part(me, a, b, u0, u1, d0, d1).astype(jnp.bfloat16))
    half = a.shape[0]
    sum_a = sum_b = None
    for step in range(1, chips):
        a, b = a1, b1
        if step < chips - 1:
            a1, b1 = hop(a, 1), hop(b, -1)
        part = expert_part(me, a, b, u0, u1, d0, d1)
        part_a, part_b = part[:half], part[half:]
        if step > 1:
            part_a = part_a + sum_a.astype(jnp.float32)
            part_b = part_b + sum_b.astype(jnp.float32)
        move = hop if step < chips - 1 else last_hop
        sum_a = move(part_a.astype(jnp.bfloat16), 1)
        sum_b = move(part_b.astype(jnp.bfloat16), -1)
    return finish(x_out, grad_out, gain_out, own, sum_a, sum_b)[None]


def solution(mesh):
    return jax.shard_map(
        shards,
        mesh=mesh,
        in_specs=(
            P("pipe", "expert", None),
            P("pipe", "expert", None),
            P("pipe", None),
            P("pipe", "expert", None, None),
            P("pipe", "expert", None, None),
            P("pipe", "expert", None),
            P("pipe", "expert", None),
        ),
        out_specs=P("pipe", "expert", None),
        check_vma=False,
    )
```

```python
import jax
import jax.numpy as jnp
from jax import lax
from jax.experimental import pallas as pl
from jax.experimental.pallas import tpu as pltpu
from jax.sharding import PartitionSpec as P

epsilon = 1e-06
LANES = 128
NT = (((1,), (1,)), ((), ()))


def pack_kernel(x_ref, g_ref, gain_ref, routes_ref, gates_ref, up_ref, down_ref):
    half, width = up_ref.shape[0], x_ref.shape[1]
    values = x_ref[...].astype(jnp.float32)
    scaling = lax.rsqrt(jnp.mean(values * values, axis=-1, keepdims=True) + epsilon)
    normed = (values * scaling * gain_ref[...]).astype(jnp.bfloat16)
    lanes = up_ref.shape[1] - 2 * width
    lane = lax.broadcasted_iota(jnp.int32, (x_ref.shape[0], lanes), 1)
    dense = jnp.zeros((x_ref.shape[0], lanes), jnp.float32)
    routes, gates = routes_ref[...], gates_ref[...].astype(jnp.float32)
    for k in range(routes.shape[1]):
        dense = dense + jnp.where(lane == routes[:, k : k + 1], gates[:, k : k + 1], 0.0)
    dense = dense.astype(jnp.bfloat16)
    for ref, first in ((up_ref, 0), (down_ref, half)):
        ref[:, :width] = normed[first : first + half]
        ref[:, width : 2 * width] = g_ref[first : first + half, :]
        ref[:, 2 * width :] = dense[first : first + half]


def pack(x, grad, gain, routes, gates, experts):
    rows, width = x.shape
    lanes = -(-experts // LANES) * LANES
    shape = jax.ShapeDtypeStruct((rows // 2, 2 * width + lanes), jnp.bfloat16)
    return pl.pallas_call(
        pack_kernel,
        out_shape=(shape, shape),
        compiler_params=pltpu.CompilerParams(vmem_limit_bytes=40 << 20),
        name="pack",
    )(x, grad, gain, routes, gates)


def expert_kernel(me_ref, a_ref, b_ref, u0_ref, u1_ref, d0_ref, d1_ref, o_ref):
    width = u0_ref.shape[0]

    def rows(first, last):
        return jnp.concatenate([a_ref[:, first:last], b_ref[:, first:last]], axis=0)

    normed, grad = rows(0, width), rows(width, 2 * width)
    dense = rows(2 * width, a_ref.shape[1]).astype(jnp.float32)
    lane = lax.broadcasted_iota(jnp.int32, dense.shape, 1)
    for i, (u_ref, d_ref) in enumerate(((u0_ref, d0_ref), (u1_ref, d1_ref))):
        before = jnp.dot(normed, u_ref[...], preferred_element_type=jnp.float32)
        d_hidden = lax.dot_general(grad, d_ref[...], NT, preferred_element_type=jnp.float32)
        sigmoid_of = jax.nn.sigmoid(before)
        d_before = (d_hidden * sigmoid_of * (1.0 + before * (1.0 - sigmoid_of))).astype(jnp.bfloat16)
        d_route = lax.dot_general(d_before, u_ref[...], NT, preferred_element_type=jnp.float32)
        gate = jnp.sum(jnp.where(lane == me_ref[i], dense, 0.0), axis=-1, keepdims=True)
        part = d_route.astype(jnp.bfloat16).astype(jnp.float32) * gate
        if i == 0:
            o_ref[...] = part
        else:
            o_ref[...] += part


def expert_part(me, a, b, u0, u1, d0, d1):
    half = a.shape[0]
    width, hidden = u0.shape
    whole = pl.BlockSpec(memory_space=pltpu.VMEM)
    return pl.pallas_call(
        expert_kernel,
        out_shape=jax.ShapeDtypeStruct((2 * half, width), jnp.float32),
        in_specs=[pl.BlockSpec(memory_space=pltpu.SMEM)] + [whole] * 6,
        out_specs=whole,
        compiler_params=pltpu.CompilerParams(vmem_limit_bytes=30 << 20),
        cost_estimate=pl.CostEstimate(
            flops=24 * half * width * hidden,
            transcendentals=4 * half * hidden,
            bytes_accessed=8 * width * hidden + 12 * half * width,
        ),
        name="expert_part",
    )(me, a, b, u0, u1, d0, d1)


def finish_kernel(x_ref, g_ref, gain_ref, own_ref, a_ref, b_ref, o_ref):
    half = a_ref.shape[0]
    for ref, first in ((a_ref, 0), (b_ref, half)):
        part = slice(first, first + half)
        values = x_ref[part, :].astype(jnp.float32)
        scaling = lax.rsqrt(jnp.mean(values * values, axis=-1, keepdims=True) + epsilon)
        d_normed = own_ref[part, :].astype(jnp.float32) + ref[...].astype(jnp.float32)
        weighted = gain_ref[...] * d_normed
        inner_mean = jnp.mean(values * weighted, axis=-1, keepdims=True)
        back = scaling * weighted - values * (scaling * scaling * scaling) * inner_mean
        o_ref[part, :] = (g_ref[part, :].astype(jnp.float32) + back).astype(jnp.bfloat16)


def finish(x, grad, gain, own, a, b):
    return pl.pallas_call(
        finish_kernel,
        out_shape=jax.ShapeDtypeStruct(x.shape, jnp.bfloat16),
        compiler_params=pltpu.CompilerParams(vmem_limit_bytes=40 << 20),
        name="finish",
    )(x, grad, gain, own, a, b)


def shards(bwd_input, out_grad, norm_gain, up_weight, down_weight, bwd_routes, bwd_gates):
    experts = lax.axis_size("expert")
    sections = lax.axis_size("pipe")
    chips = experts // 2
    ring = list(range(0, chips, 2)) + list(range(1, chips, 2))[::-1]

    def hop(value, by):
        moves = [(ring[i], ring[(i + by) % chips]) for i in range(chips)]
        return lax.ppermute(value, "expert", [(2 * a + c, 2 * b + c) for a, b in moves for c in (0, 1)])

    def last_hop(value, by):
        moves = [(ring[i], ring[(i + by) % chips]) for i in range(chips)]
        return lax.ppermute(
            value,
            ("pipe", "expert"),
            [
                (s * experts + 2 * a + c, (s - 1) % sections * experts + 2 * b + c)
                for s in range(sections)
                for a, b in moves
                for c in (0, 1)
            ],
        )

    def to_previous(value):
        return lax.ppermute(value, "pipe", [(s, (s - 1) % sections) for s in range(sections)])

    def swap(value):
        return lax.ppermute(value, "expert", [(e, e ^ 1) for e in range(experts)])

    x, grad = bwd_input[0], out_grad[0]
    u0, d0 = up_weight[0, 0], down_weight[0, 0]
    e = lax.axis_index("expert").astype(jnp.int32)
    me = jnp.stack([e, e ^ 1])

    u1, d1 = swap(u0), swap(d0)
    a, b = pack(x, grad, norm_gain, bwd_routes[0], bwd_gates[0], experts)
    half = a.shape[0]
    a1, b1 = hop(a, 1), hop(b, -1)
    x_out, grad_out, gain_out = to_previous(x), to_previous(grad), to_previous(norm_gain)
    own = expert_part(me, a, b, u0, u1, d0, d1).astype(jnp.bfloat16)
    own_out = to_previous(own)
    sum_a = sum_b = None
    for step in range(1, chips):
        a, b = a1, b1
        if step == 1:
            a, b, own = lax.optimization_barrier((a, b, own))
        if step == 3:
            a, b, x_out, grad_out, gain_out = lax.optimization_barrier((a, b, x_out, grad_out, gain_out))
        if step == 5:
            a, b, own_out = lax.optimization_barrier((a, b, own_out))
        if step < chips - 1:
            a1, b1 = hop(a, 1), hop(b, -1)
        part = expert_part(me, a, b, u0, u1, d0, d1)
        part_a, part_b = part[:half], part[half:]
        if step > 1:
            part_a = part_a + sum_a.astype(jnp.float32)
            part_b = part_b + sum_b.astype(jnp.float32)
        move = hop if step < chips - 1 else last_hop
        sum_a = move(part_a.astype(jnp.bfloat16), 1)
        sum_b = move(part_b.astype(jnp.bfloat16), -1)
    return finish(x_out, grad_out, gain_out, own_out, sum_a, sum_b)[None]


def solution(mesh):
    return jax.shard_map(
        shards,
        mesh=mesh,
        in_specs=(
            P("pipe", "expert", None),
            P("pipe", "expert", None),
            P("pipe", None),
            P("pipe", "expert", None, None),
            P("pipe", "expert", None, None),
            P("pipe", "expert", None),
            P("pipe", "expert", None),
        ),
        out_specs=P("pipe", "expert", None),
        check_vma=False,
    )
```

```python
import functools

import jax
import jax.numpy as jnp
from jax import lax
from jax.experimental import pallas as pl
from jax.experimental.pallas import tpu as pltpu
from jax.sharding import PartitionSpec as P

epsilon = 1e-06
LANES = 128
VMEM = 24 << 20
NT = (((1,), (1,)), ((), ()))


def pack_kernel(x_ref, gain_ref, routes_ref, gates_ref, up_ref, down_ref):
    half = up_ref.shape[0]
    rows, width = x_ref.shape
    values = x_ref[...].astype(jnp.float32)
    scaling = lax.rsqrt(jnp.mean(values * values, axis=-1, keepdims=True) + epsilon)
    normed = (values * scaling * gain_ref[...]).astype(jnp.bfloat16)
    expert = lax.broadcasted_iota(jnp.int32, (up_ref.shape[1] - width, rows), 0)
    dense = jnp.zeros(expert.shape, jnp.float32)
    routes, gates = routes_ref[...], gates_ref[...].astype(jnp.float32)
    for k in range(routes.shape[0]):
        dense = dense + jnp.where(expert == routes[k : k + 1, :], gates[k : k + 1, :], 0.0)
    dense = dense.T.astype(jnp.bfloat16)
    for ref, first in ((up_ref, 0), (down_ref, half)):
        ref[:, :width] = normed[first : first + half]
        ref[:, width:] = dense[first : first + half]


def pack(x, gain, routes, gates, experts):
    rows, width = x.shape
    lanes = -(-experts // LANES) * LANES
    shape = jax.ShapeDtypeStruct((rows // 2, width + lanes), jnp.bfloat16)
    return pl.pallas_call(
        pack_kernel,
        out_shape=(shape, shape),
        compiler_params=pltpu.CompilerParams(vmem_limit_bytes=VMEM),
        name="pack",
    )(x, gain, routes.T, gates.T)


def expert_kernel(pieces, me_ref, *refs):
    rows, (u0_ref, u1_ref, d0_hbm, d1_hbm, o_ref, d0_ref, d1_ref, sems) = refs[: 2 * pieces], refs[2 * pieces :]
    copies = [
        pltpu.make_async_copy(hbm, vmem, sems.at[i])
        for i, (hbm, vmem) in enumerate(((d0_hbm, d0_ref), (d1_hbm, d1_ref)))
    ]
    for copy in copies:
        copy.start()
    width = u0_ref.shape[0]
    split = rows[0].shape[1] - (width if pieces == 1 else 0)
    heads = rows[:2]
    normed = jnp.concatenate([ref[:, :width] for ref in heads], axis=0)
    dense = jnp.concatenate([ref[:, width:split] for ref in heads], axis=0).astype(jnp.float32)
    tails = [ref[:, split:] for ref in heads] if pieces == 1 else [ref[...] for ref in rows[2:]]
    grad = jnp.concatenate(tails, axis=0)
    lane = lax.broadcasted_iota(jnp.int32, dense.shape, 1)
    for i, (u_ref, d_ref) in enumerate(((u0_ref, d0_ref), (u1_ref, d1_ref))):
        before = jnp.dot(normed, u_ref[...], preferred_element_type=jnp.float32)
        copies[i].wait()
        d_hidden = lax.dot_general(grad, d_ref[...], NT, preferred_element_type=jnp.float32)
        sigmoid_of = jax.nn.sigmoid(before)
        d_before = (d_hidden * sigmoid_of * (1.0 + before * (1.0 - sigmoid_of))).astype(jnp.bfloat16)
        d_route = lax.dot_general(d_before, u_ref[...], NT, preferred_element_type=jnp.float32)
        gate = jnp.sum(jnp.where(lane == me_ref[i], dense, 0.0), axis=-1, keepdims=True)
        part = d_route.astype(jnp.bfloat16).astype(jnp.float32) * gate
        if i == 0:
            o_ref[...] = part
        else:
            o_ref[...] += part


def expert_part(me, rows, weights):
    half = rows[0].shape[0]
    width, hidden = weights[0].shape
    whole, stay = pl.BlockSpec(memory_space=pltpu.VMEM), pl.BlockSpec(memory_space=pl.ANY)
    return pl.pallas_call(
        functools.partial(expert_kernel, len(rows) // 2),
        out_shape=jax.ShapeDtypeStruct((2 * half, width), jnp.float32),
        in_specs=[pl.BlockSpec(memory_space=pltpu.SMEM)] + [whole] * (len(rows) + 2) + [stay] * 2,
        out_specs=whole,
        scratch_shapes=[
            pltpu.VMEM((hidden, width), jnp.bfloat16),
            pltpu.VMEM((hidden, width), jnp.bfloat16),
            pltpu.SemaphoreType.DMA((2,)),
        ],
        compiler_params=pltpu.CompilerParams(vmem_limit_bytes=VMEM),
        cost_estimate=pl.CostEstimate(
            flops=24 * half * width * hidden,
            transcendentals=4 * half * hidden,
            bytes_accessed=8 * width * hidden + 12 * half * width,
        ),
        name="expert_part",
    )(me, *rows, *weights)


def finish_kernel(x_ref, g_ref, gain_ref, own_ref, a_ref, b_ref, o_ref):
    half = a_ref.shape[0]
    for ref, first in ((a_ref, 0), (b_ref, half)):
        part = slice(first, first + half)
        values = x_ref[part, :].astype(jnp.float32)
        scaling = lax.rsqrt(jnp.mean(values * values, axis=-1, keepdims=True) + epsilon)
        d_normed = own_ref[part, :].astype(jnp.float32) + ref[...].astype(jnp.float32)
        weighted = gain_ref[...] * d_normed
        inner_mean = jnp.mean(values * weighted, axis=-1, keepdims=True)
        back = scaling * weighted - values * (scaling * scaling * scaling) * inner_mean
        o_ref[part, :] = (g_ref[part, :].astype(jnp.float32) + back).astype(jnp.bfloat16)


def finish(x, grad, gain, own, a, b):
    return pl.pallas_call(
        finish_kernel,
        out_shape=jax.ShapeDtypeStruct(x.shape, jnp.bfloat16),
        compiler_params=pltpu.CompilerParams(vmem_limit_bytes=VMEM),
        name="finish",
    )(x, grad, gain, own, a, b)


def shards(bwd_input, out_grad, norm_gain, up_weight, down_weight, bwd_routes, bwd_gates):
    experts = lax.axis_size("expert")
    sections = lax.axis_size("pipe")
    chips = experts // 2
    ring = list(range(0, chips, 2)) + list(range(1, chips, 2))[::-1]

    def hop(value, by):
        moves = [(ring[i], ring[(i + by) % chips]) for i in range(chips)]
        return lax.ppermute(value, "expert", [(2 * a + c, 2 * b + c) for a, b in moves for c in (0, 1)])

    def last_hop(value, by):
        moves = [(ring[i], ring[(i + by) % chips]) for i in range(chips)]
        return lax.ppermute(
            value,
            ("pipe", "expert"),
            [
                (s * experts + 2 * a + c, (s - 1) % sections * experts + 2 * b + c)
                for s in range(sections)
                for a, b in moves
                for c in (0, 1)
            ],
        )

    def to_previous(value):
        return lax.ppermute(value, "pipe", [(s, (s - 1) % sections) for s in range(sections)])

    def swap(value):
        return lax.ppermute(value, "expert", [(e, e ^ 1) for e in range(experts)])

    x, grad = bwd_input[0], out_grad[0]
    u0, d0 = up_weight[0, 0], down_weight[0, 0]
    e = lax.axis_index("expert").astype(jnp.int32)
    me = jnp.stack([e, e ^ 1])

    half = grad.shape[0] // 2
    ga, gb = grad[:half], grad[half:]
    ga1, gb1 = hop(ga, 1), hop(gb, -1)
    weights = (u0, swap(u0), d0, swap(d0))
    na, nb = pack(x, norm_gain, bwd_routes[0], bwd_gates[0], experts)
    na1, nb1 = hop(na, 1), hop(nb, -1)
    a1, b1 = jnp.concatenate([na1, ga1], axis=1), jnp.concatenate([nb1, gb1], axis=1)
    x_out, grad_out, gain_out = to_previous(x), to_previous(grad), to_previous(norm_gain)
    own = expert_part(me, (na, nb, ga, gb), weights).astype(jnp.bfloat16)
    own_out = to_previous(own)
    early = {2: gain_out, 3: x_out, 4: grad_out, 5: own, 7: own_out}
    sum_a = sum_b = None
    for step in range(1, chips):
        a, b = a1, b1
        if step in early:
            a, b, early[step] = lax.optimization_barrier((a, b, early[step]))
        if step < chips - 1:
            a1, b1 = hop(a, 1), hop(b, -1)
        part = expert_part(me, (a, b), weights)
        part_a, part_b = part[:half], part[half:]
        if step > 1:
            part_a = part_a + sum_a.astype(jnp.float32)
            part_b = part_b + sum_b.astype(jnp.float32)
        send_a, send_b = part_a.astype(jnp.bfloat16), part_b.astype(jnp.bfloat16)
        if step == chips - 2:
            a1, b1, send_a, send_b = lax.optimization_barrier((a1, b1, send_a, send_b))
        move = hop if step < chips - 1 else last_hop
        sum_a, sum_b = move(send_a, 1), move(send_b, -1)
    return finish(x_out, grad_out, gain_out, own_out, sum_a, sum_b)[None]


def solution(mesh):
    return jax.shard_map(
        shards,
        mesh=mesh,
        in_specs=(
            P("pipe", "expert", None),
            P("pipe", "expert", None),
            P("pipe", None),
            P("pipe", "expert", None, None),
            P("pipe", "expert", None, None),
            P("pipe", "expert", None),
            P("pipe", "expert", None),
        ),
        out_specs=P("pipe", "expert", None),
        check_vma=False,
    )
```

```python
import jax
import jax.numpy as jnp
from jax import lax
from jax.experimental import pallas as pl
from jax.experimental.pallas import tpu as pltpu
from jax.sharding import PartitionSpec as P

epsilon = 1e-06
LANES = 128
VMEM = 16 << 20
NT = (((1,), (1,)), ((), ()))


def pack_kernel(x_hbm, grad_hbm, gain_hbm, routes_hbm, gates_hbm, a_ref, b_ref, keep_hbm, keep_ref, grad_s, gain_s, routes_s, gates_s, sems):
    half = a_ref.shape[0]
    rows, width = x_hbm.shape
    x_ref = keep_ref.at[pl.ds(0, rows)]
    copies = [
        pltpu.make_async_copy(hbm, vmem, sems.at[i])
        for i, (hbm, vmem) in enumerate(
            ((x_hbm, x_ref), (gain_hbm, gain_s), (routes_hbm, routes_s), (gates_hbm, gates_s), (grad_hbm, grad_s))
        )
    ]
    for copy in copies:
        copy.start()
    for copy in copies[:4]:
        copy.wait()
    gain = gain_s[...]
    values = x_ref[...].astype(jnp.float32)
    scaling = lax.rsqrt(jnp.mean(values * values, axis=-1, keepdims=True) + epsilon)
    normed = (values * scaling * gain).astype(jnp.bfloat16)
    expert = lax.broadcasted_iota(jnp.int32, (a_ref.shape[1] - 2 * width, rows), 0)
    dense = jnp.zeros(expert.shape, jnp.float32)
    routes, gates = routes_s[...], gates_s[...].astype(jnp.float32)
    for k in range(routes.shape[0]):
        dense = dense + jnp.where(expert == routes[k : k + 1, :], gates[k : k + 1, :], 0.0)
    dense = dense.T.astype(jnp.bfloat16)
    high = gain.astype(jnp.bfloat16).astype(jnp.float32)
    middle = (gain - high).astype(jnp.bfloat16).astype(jnp.float32)
    low = gain - high - middle
    row = lax.broadcasted_iota(jnp.int32, (keep_ref.shape[0] - rows, width), 0)
    pieces = jnp.where(row == 0, high, jnp.where(row == 1, middle, jnp.where(row == 2, low, 0.0)))
    keep_ref[rows:, :] = pieces.astype(jnp.bfloat16)
    kept = pltpu.make_async_copy(keep_ref, keep_hbm, sems.at[5])
    kept.start()
    copies[4].wait()
    for ref, first in ((a_ref, 0), (b_ref, half)):
        ref[:, :width] = normed[first : first + half]
        ref[:, width:-width] = dense[first : first + half]
        ref[:, -width:] = grad_s[first : first + half, :]
    kept.wait()


def pack(x, grad, gain, routes, gates, experts):
    rows, width = x.shape
    top = routes.shape[1]
    lanes = -(-experts // LANES) * LANES
    shape = pltpu.VMEM((rows // 2, 2 * width + lanes), jnp.bfloat16)
    args = (x, grad, gain, routes.T, gates.T)
    return pl.pallas_call(
        pack_kernel,
        out_shape=(shape, shape, pltpu.HBM((rows + 16, width), jnp.bfloat16)),
        in_specs=[pl.BlockSpec(memory_space=pltpu.HBM)] * 5,
        out_specs=(pl.BlockSpec(memory_space=pltpu.VMEM),) * 2 + (pl.BlockSpec(memory_space=pltpu.HBM),),
        scratch_shapes=[
            pltpu.VMEM((rows + 16, width), jnp.bfloat16),
            pltpu.VMEM((rows, width), jnp.bfloat16),
            pltpu.VMEM((1, width), jnp.float32),
            pltpu.VMEM((top, rows), jnp.int32),
            pltpu.VMEM((top, rows), jnp.bfloat16),
            pltpu.SemaphoreType.DMA((6,)),
        ],
        compiler_params=pltpu.CompilerParams(vmem_limit_bytes=VMEM),
        name="pack",
    )(*(pltpu.with_memory_space_constraint(value, pltpu.HBM) for value in args))


def hold_kernel(up_hbm, down_hbm, up_ref, down_ref, sems):
    copies = [pltpu.make_async_copy(up_hbm, up_ref, sems.at[0]), pltpu.make_async_copy(down_hbm, down_ref, sems.at[1])]
    for copy in copies:
        copy.start()
    for copy in copies:
        copy.wait()


def hold(up, down):
    return pl.pallas_call(
        hold_kernel,
        out_shape=(pltpu.VMEM(up.shape, up.dtype), pltpu.VMEM(down.shape, down.dtype)),
        in_specs=[pl.BlockSpec(memory_space=pltpu.HBM)] * 2,
        out_specs=(pl.BlockSpec(memory_space=pltpu.VMEM),) * 2,
        scratch_shapes=[pltpu.SemaphoreType.DMA((2,))],
        compiler_params=pltpu.CompilerParams(vmem_limit_bytes=1 << 20),
        name="hold",
    )(*(pltpu.with_memory_space_constraint(value, pltpu.HBM) for value in (up, down)))


def expert_kernel(me_ref, a_ref, b_ref, u0_ref, d0_ref, u1_ref, d1_ref, o_ref):
    width = u0_ref.shape[0]

    def rows(first, last):
        return jnp.concatenate([a_ref[:, first:last], b_ref[:, first:last]], axis=0)

    last = a_ref.shape[1]
    normed, dense, grad = rows(0, width), rows(width, last - width).astype(jnp.float32), rows(last - width, last)
    lane = lax.broadcasted_iota(jnp.int32, dense.shape, 1)
    for i, (u_ref, d_ref) in enumerate(((u0_ref, d0_ref), (u1_ref, d1_ref))):
        before = jnp.dot(normed, u_ref[...], preferred_element_type=jnp.float32)
        d_hidden = lax.dot_general(grad, d_ref[...], NT, preferred_element_type=jnp.float32)
        sigmoid_of = jax.nn.sigmoid(before)
        d_before = (d_hidden * sigmoid_of * (1.0 + before * (1.0 - sigmoid_of))).astype(jnp.bfloat16)
        d_route = lax.dot_general(d_before, u_ref[...], NT, preferred_element_type=jnp.float32)
        gate = jnp.sum(jnp.where(lane == me_ref[i], dense, 0.0), axis=-1, keepdims=True)
        part = d_route.astype(jnp.bfloat16).astype(jnp.float32) * gate
        if i == 0:
            o_ref[...] = part
        else:
            o_ref[...] += part


def expert_part(me, a, b, weights):
    half = a.shape[0]
    width, hidden = weights[0].shape
    whole = pl.BlockSpec(memory_space=pltpu.VMEM)
    return pl.pallas_call(
        expert_kernel,
        out_shape=jax.ShapeDtypeStruct((2 * half, width), jnp.float32),
        in_specs=[pl.BlockSpec(memory_space=pltpu.SMEM)] + [whole] * 6,
        out_specs=whole,
        compiler_params=pltpu.CompilerParams(vmem_limit_bytes=VMEM),
        cost_estimate=pl.CostEstimate(
            flops=24 * half * width * hidden,
            transcendentals=4 * half * hidden,
            bytes_accessed=8 * width * hidden + 12 * half * width,
        ),
        name="expert_part",
    )(me, a, b, *weights)


def finish_kernel(keep_ref, g_ref, own_ref, a_ref, b_ref, o_ref):
    half = a_ref.shape[0]
    rows = 2 * half
    pieces = keep_ref[rows : rows + 16, :].astype(jnp.float32)
    gain = (pieces[0:1, :] + pieces[1:2, :]) + pieces[2:3, :]
    for ref, first in ((a_ref, 0), (b_ref, half)):
        part = slice(first, first + half)
        values = keep_ref[part, :].astype(jnp.float32)
        scaling = lax.rsqrt(jnp.mean(values * values, axis=-1, keepdims=True) + epsilon)
        d_normed = own_ref[part, :].astype(jnp.float32) + ref[...].astype(jnp.float32)
        weighted = gain * d_normed
        inner_mean = jnp.mean(values * weighted, axis=-1, keepdims=True)
        back = scaling * weighted - values * (scaling * scaling * scaling) * inner_mean
        o_ref[part, :] = (g_ref[part, :].astype(jnp.float32) + back).astype(jnp.bfloat16)


def finish(keep, grad, own, a, b):
    return pl.pallas_call(
        finish_kernel,
        out_shape=jax.ShapeDtypeStruct(grad.shape, jnp.bfloat16),
        compiler_params=pltpu.CompilerParams(vmem_limit_bytes=VMEM),
        name="finish",
    )(keep, grad, own, a, b)


def shards(bwd_input, out_grad, norm_gain, up_weight, down_weight, bwd_routes, bwd_gates):
    experts = lax.axis_size("expert")
    sections = lax.axis_size("pipe")
    chips = experts // 2
    ring = list(range(0, chips, 2)) + list(range(1, chips, 2))[::-1]

    def hop(value, by):
        moves = [(ring[i], ring[(i + by) % chips]) for i in range(chips)]
        return lax.ppermute(value, "expert", [(2 * a + c, 2 * b + c) for a, b in moves for c in (0, 1)])

    def last_hop(value, by):
        moves = [(ring[i], ring[(i + by) % chips]) for i in range(chips)]
        return lax.ppermute(
            value,
            ("pipe", "expert"),
            [
                (s * experts + 2 * a + c, (s - 1) % sections * experts + 2 * b + c)
                for s in range(sections)
                for a, b in moves
                for c in (0, 1)
            ],
        )

    def to_previous(value):
        return lax.ppermute(value, "pipe", [(s, (s - 1) % sections) for s in range(sections)])

    def swap(value):
        return lax.ppermute(value, "expert", [(e, e ^ 1) for e in range(experts)])

    x, grad = bwd_input[0], out_grad[0]
    u0, d0 = up_weight[0, 0], down_weight[0, 0]
    e = lax.axis_index("expert").astype(jnp.int32)
    me = jnp.stack([e, e ^ 1])

    half = grad.shape[0] // 2
    u1, d1 = swap(u0), swap(d0)
    a, b, keep = pack(x, grad, norm_gain, bwd_routes[0], bwd_gates[0], experts)
    a1, b1 = hop(a, 1), hop(b, -1)
    weights = (*hold(u0, d0), *hold(u1, d1))
    own = expert_part(me, a, b, weights).astype(jnp.bfloat16)
    own_out, keep_out, grad_out = to_previous(own), to_previous(keep), to_previous(grad)
    early = {3: own, 2: keep_out, 4: grad_out, 6: own_out}
    sum_a = sum_b = None
    for step in range(1, chips):
        a, b = a1, b1
        if step in early:
            a, b, early[step] = lax.optimization_barrier((a, b, early[step]))
        if step < chips - 1:
            a1, b1 = hop(a, 1), hop(b, -1)
        part = expert_part(me, a, b, weights)
        part_a, part_b = part[:half], part[half:]
        if step > 1:
            part_a = part_a + sum_a.astype(jnp.float32)
            part_b = part_b + sum_b.astype(jnp.float32)
        send_a, send_b = part_a.astype(jnp.bfloat16), part_b.astype(jnp.bfloat16)
        if step == chips - 2:
            a1, b1, send_a, send_b = lax.optimization_barrier((a1, b1, send_a, send_b))
        move = hop if step < chips - 1 else last_hop
        sum_a, sum_b = move(send_a, 1), move(send_b, -1)
    return finish(keep_out, grad_out, own_out, sum_a, sum_b)[None]


def solution(mesh):
    return jax.shard_map(
        shards,
        mesh=mesh,
        in_specs=(
            P("pipe", "expert", None),
            P("pipe", "expert", None),
            P("pipe", None),
            P("pipe", "expert", None, None),
            P("pipe", "expert", None, None),
            P("pipe", "expert", None),
            P("pipe", "expert", None),
        ),
        out_specs=P("pipe", "expert", None),
        check_vma=False,
    )
```

```python
import jax
import jax.numpy as jnp
from jax import lax
from jax.experimental import pallas as pl
from jax.experimental.pallas import tpu as pltpu
from jax.sharding import PartitionSpec as P

epsilon = 1e-06
LANES = 128
VMEM = 16 << 20
NT = (((1,), (1,)), ((), ()))


def pack_kernel(x_hbm, grad_hbm, gain_hbm, routes_hbm, gates_hbm, a_ref, b_ref, keep_ref, grad_s, gain_s, routes_s, gates_s, sems):
    rows, width = x_hbm.shape
    half, slabs = rows // 2, width // LANES
    x_ref = keep_ref.at[pl.ds(0, rows)]
    copies = [
        pltpu.make_async_copy(hbm, vmem, sems.at[i])
        for i, (hbm, vmem) in enumerate(
            ((x_hbm, x_ref), (gain_hbm, gain_s), (routes_hbm, routes_s), (gates_hbm, gates_s), (grad_hbm, grad_s))
        )
    ]
    for copy in copies:
        copy.start()
    for copy in copies[:4]:
        copy.wait()
    gain = gain_s[...]
    values = x_ref[...].astype(jnp.float32)
    scaling = lax.rsqrt(jnp.mean(values * values, axis=-1, keepdims=True) + epsilon)
    normed = (values * scaling * gain).astype(jnp.bfloat16)
    shape = (a_ref.shape[0] - 2 * slabs * half, rows)
    expert = lax.broadcasted_iota(jnp.int32, shape, 0)
    dense = jnp.zeros(shape, jnp.float32)
    routes, gates = routes_s[...], gates_s[...].astype(jnp.float32)
    for k in range(routes.shape[0]):
        dense = dense + jnp.where(expert == routes[k : k + 1, :], gates[k : k + 1, :], 0.0)
    token = lax.broadcasted_iota(jnp.int32, shape, 1)
    high = gain.astype(jnp.bfloat16).astype(jnp.float32)
    middle = (gain - high).astype(jnp.bfloat16).astype(jnp.float32)
    low = gain - high - middle
    row = lax.broadcasted_iota(jnp.int32, (keep_ref.shape[0] - rows, width), 0)
    pieces = jnp.where(row == 0, high, jnp.where(row == 1, middle, jnp.where(row == 2, low, 0.0)))
    keep_ref[rows:, :] = pieces.astype(jnp.bfloat16)
    copies[4].wait()
    for ref, first in ((a_ref, 0), (b_ref, half)):
        for k in range(slabs):
            part, lanes = slice(first, first + half), slice(k * LANES, (k + 1) * LANES)
            ref[k * half : (k + 1) * half, :] = normed[part, lanes]
            ref[(slabs + k) * half : (slabs + k + 1) * half, :] = grad_s[part, lanes]
        here = (token >= first) & (token < first + half)
        ref[2 * slabs * half :, :] = jnp.where(here, dense, 0.0).astype(jnp.bfloat16)


def pack(x, grad, gain, routes, gates, experts):
    rows, width = x.shape
    top = routes.shape[1]
    shape = pltpu.VMEM((width // LANES * rows + -(-experts // 16) * 16, LANES), jnp.bfloat16)
    args = (x, grad, gain, routes.T, gates.T)
    return pl.pallas_call(
        pack_kernel,
        out_shape=(shape, shape, pltpu.VMEM((rows + 16, width), jnp.bfloat16)),
        in_specs=[pl.BlockSpec(memory_space=pltpu.HBM)] * 5,
        out_specs=(pl.BlockSpec(memory_space=pltpu.VMEM),) * 3,
        scratch_shapes=[
            pltpu.VMEM((rows, width), jnp.bfloat16),
            pltpu.VMEM((1, width), jnp.float32),
            pltpu.VMEM((top, rows), jnp.int32),
            pltpu.VMEM((top, rows), jnp.bfloat16),
            pltpu.SemaphoreType.DMA((5,)),
        ],
        compiler_params=pltpu.CompilerParams(vmem_limit_bytes=VMEM),
        name="pack",
    )(*(pltpu.with_memory_space_constraint(value, pltpu.HBM) for value in args))


def hold_kernel(*refs):
    count = len(refs) // 2
    copies = [pltpu.make_async_copy(refs[i], refs[count + i], refs[-1].at[i]) for i in range(count)]
    for copy in copies:
        copy.start()
    for copy in copies:
        copy.wait()


def hold(*values):
    return pl.pallas_call(
        hold_kernel,
        out_shape=[pltpu.VMEM(value.shape, value.dtype) for value in values],
        in_specs=[pl.BlockSpec(memory_space=pltpu.HBM)] * len(values),
        out_specs=[pl.BlockSpec(memory_space=pltpu.VMEM)] * len(values),
        scratch_shapes=[pltpu.SemaphoreType.DMA((len(values),))],
        compiler_params=pltpu.CompilerParams(vmem_limit_bytes=1 << 20),
        name="hold",
    )(*(pltpu.with_memory_space_constraint(value, pltpu.HBM) for value in values))


def expert_kernel(me_ref, a_ref, b_ref, u0_ref, d0_ref, u1_ref, d1_ref, o_ref):
    rows, width = o_ref.shape
    half, slabs = rows // 2, width // LANES

    def features(first):
        return jnp.concatenate(
            [
                jnp.concatenate([ref[k * half : (k + 1) * half, :] for k in range(first, first + slabs)], axis=1)
                for ref in (a_ref, b_ref)
            ],
            axis=0,
        )

    normed, grad = features(0), features(slabs)
    dense = sum(ref[2 * slabs * half :, :].astype(jnp.float32) for ref in (a_ref, b_ref))
    expert = lax.broadcasted_iota(jnp.int32, dense.shape, 0)
    square = (rows, rows)
    on_line = lax.broadcasted_iota(jnp.int32, square, 0) == lax.broadcasted_iota(jnp.int32, square, 1)
    for i, (u_ref, d_ref) in enumerate(((u0_ref, d0_ref), (u1_ref, d1_ref))):
        before = jnp.dot(normed, u_ref[...], preferred_element_type=jnp.float32)
        d_hidden = lax.dot_general(grad, d_ref[...], NT, preferred_element_type=jnp.float32)
        sigmoid_of = jax.nn.sigmoid(before)
        d_before = (d_hidden * sigmoid_of * (1.0 + before * (1.0 - sigmoid_of))).astype(jnp.bfloat16)
        d_route = lax.dot_general(d_before, u_ref[...], NT, preferred_element_type=jnp.float32)
        named = jnp.sum(jnp.where(expert == me_ref[i], dense, 0.0), axis=0, keepdims=True)
        gate = jnp.sum(jnp.where(on_line, jnp.broadcast_to(named, square), 0.0), axis=-1, keepdims=True)
        part = d_route.astype(jnp.bfloat16).astype(jnp.float32) * gate
        if i == 0:
            o_ref[...] = part
        else:
            o_ref[...] += part


def expert_part(me, a, b, rows, weights):
    width, hidden = weights[0].shape
    whole = pl.BlockSpec(memory_space=pltpu.VMEM)
    return pl.pallas_call(
        expert_kernel,
        out_shape=jax.ShapeDtypeStruct((rows, width), jnp.float32),
        in_specs=[pl.BlockSpec(memory_space=pltpu.SMEM)] + [whole] * 6,
        out_specs=whole,
        compiler_params=pltpu.CompilerParams(vmem_limit_bytes=VMEM),
        cost_estimate=pl.CostEstimate(
            flops=12 * rows * width * hidden,
            transcendentals=2 * rows * hidden,
            bytes_accessed=8 * width * hidden + 8 * rows * width,
        ),
        name="expert_part",
    )(me, a, b, *weights)


def finish_kernel(keep_ref, g_ref, own_ref, a_ref, b_ref, o_ref):
    half = a_ref.shape[0]
    rows = 2 * half
    pieces = keep_ref[rows : rows + 16, :].astype(jnp.float32)
    gain = (pieces[0:1, :] + pieces[1:2, :]) + pieces[2:3, :]
    for ref, first in ((a_ref, 0), (b_ref, half)):
        part = slice(first, first + half)
        values = keep_ref[part, :].astype(jnp.float32)
        scaling = lax.rsqrt(jnp.mean(values * values, axis=-1, keepdims=True) + epsilon)
        d_normed = own_ref[part, :].astype(jnp.float32) + ref[...].astype(jnp.float32)
        weighted = gain * d_normed
        inner_mean = jnp.mean(values * weighted, axis=-1, keepdims=True)
        back = scaling * weighted - values * (scaling * scaling * scaling) * inner_mean
        o_ref[part, :] = (g_ref[part, :].astype(jnp.float32) + back).astype(jnp.bfloat16)


def finish(keep, grad, own, a, b):
    return pl.pallas_call(
        finish_kernel,
        out_shape=jax.ShapeDtypeStruct(grad.shape, jnp.bfloat16),
        compiler_params=pltpu.CompilerParams(vmem_limit_bytes=VMEM),
        name="finish",
    )(keep, grad, own, a, b)


def shards(bwd_input, out_grad, norm_gain, up_weight, down_weight, bwd_routes, bwd_gates):
    experts = lax.axis_size("expert")
    sections = lax.axis_size("pipe")
    chips = experts // 2
    ring = list(range(0, chips, 2)) + list(range(1, chips, 2))[::-1]

    def hop(value, by):
        moves = [(ring[i], ring[(i + by) % chips]) for i in range(chips)]
        return lax.ppermute(value, "expert", [(2 * a + c, 2 * b + c) for a, b in moves for c in (0, 1)])

    def last_hop(value, by):
        moves = [(ring[i], ring[(i + by) % chips]) for i in range(chips)]
        return lax.ppermute(
            value,
            ("pipe", "expert"),
            [
                (s * experts + 2 * a + c, (s - 1) % sections * experts + 2 * b + c)
                for s in range(sections)
                for a, b in moves
                for c in (0, 1)
            ],
        )

    def to_previous(value):
        return lax.ppermute(value, "pipe", [(s, (s - 1) % sections) for s in range(sections)])

    def swap(value):
        return lax.ppermute(value, "expert", [(e, e ^ 1) for e in range(experts)])

    x, grad = bwd_input[0], out_grad[0]
    u0, d0 = up_weight[0, 0], down_weight[0, 0]
    e = lax.axis_index("expert").astype(jnp.int32)
    me = jnp.stack([e, e ^ 1])

    half = grad.shape[0] // 2
    u1, d1 = swap(u0), swap(d0)
    a, b, keep = pack(x, grad, norm_gain, bwd_routes[0], bwd_gates[0], experts)
    a1, b1 = hop(a, 1), hop(b, -1)
    weights = (*hold(u0, d0), *hold(u1, d1))
    own = expert_part(me, a, b, 2 * half, weights).astype(jnp.bfloat16)
    own_out, keep_out, grad_out = to_previous(own), to_previous(keep), to_previous(grad)
    early = {3: own, 2: keep_out, 5: grad_out, 6: own_out}
    sum_a = sum_b = None
    for step in range(1, chips):
        a, b = a1, b1
        if step in early:
            a, b, early[step] = lax.optimization_barrier((a, b, early[step]))
        if step < chips - 1:
            a1, b1 = hop(a, 1), hop(b, -1)
        part = expert_part(me, a, b, 2 * half, weights)
        part_a, part_b = part[:half], part[half:]
        if step > 1:
            part_a = part_a + sum_a.astype(jnp.float32)
            part_b = part_b + sum_b.astype(jnp.float32)
        send_a, send_b = part_a.astype(jnp.bfloat16), part_b.astype(jnp.bfloat16)
        if step == chips - 2:
            a1, send_a = lax.optimization_barrier((a1, send_a))
            b1, send_b = lax.optimization_barrier((b1, send_b))
        move = hop if step < chips - 1 else last_hop
        sum_a, sum_b = move(send_a, 1), move(send_b, -1)
    held = hold(keep_out, grad_out, own_out)
    return finish(*held, sum_a, sum_b)[None]


def solution(mesh):
    return jax.shard_map(
        shards,
        mesh=mesh,
        in_specs=(
            P("pipe", "expert", None),
            P("pipe", "expert", None),
            P("pipe", None),
            P("pipe", "expert", None, None),
            P("pipe", "expert", None, None),
            P("pipe", "expert", None),
            P("pipe", "expert", None),
        ),
        out_specs=P("pipe", "expert", None),
        check_vma=False,
    )
```

```python
import jax
import jax.numpy as jnp
from jax import lax
from jax.experimental import pallas as pl
from jax.experimental.pallas import tpu as pltpu
from jax.sharding import PartitionSpec as P

epsilon = 1e-06
LANES = 128
VMEM = 16 << 20


def pack_kernel(x_hbm, grad_hbm, gain_hbm, routes_hbm, gates_hbm, a_ref, b_ref, keep_ref, grad_s, gain_s, routes_s, gates_s, sems):
    rows, width = x_hbm.shape
    half, slabs = rows // 2, width // LANES
    x_ref = keep_ref.at[pl.ds(0, rows)]
    copies = [
        pltpu.make_async_copy(hbm, vmem, sems.at[i])
        for i, (hbm, vmem) in enumerate(
            ((x_hbm, x_ref), (gain_hbm, gain_s), (routes_hbm, routes_s), (gates_hbm, gates_s), (grad_hbm, grad_s))
        )
    ]
    for copy in copies:
        copy.start()
    for copy in copies[:4]:
        copy.wait()
    gain = gain_s[...]
    values = x_ref[...].astype(jnp.float32)
    scaling = lax.rsqrt(jnp.mean(values * values, axis=-1, keepdims=True) + epsilon)
    normed = (values * scaling * gain).astype(jnp.bfloat16)
    shape = (a_ref.shape[0] - 2 * slabs * half, rows)
    expert = lax.broadcasted_iota(jnp.int32, shape, 0)
    dense = jnp.zeros(shape, jnp.float32)
    routes, gates = routes_s[...], gates_s[...].astype(jnp.float32)
    for k in range(routes.shape[0]):
        dense = dense + jnp.where(expert == routes[k : k + 1, :], gates[k : k + 1, :], 0.0)
    token = lax.broadcasted_iota(jnp.int32, shape, 1)
    high = gain.astype(jnp.bfloat16).astype(jnp.float32)
    middle = (gain - high).astype(jnp.bfloat16).astype(jnp.float32)
    low = gain - high - middle
    row = lax.broadcasted_iota(jnp.int32, (keep_ref.shape[0] - rows, width), 0)
    pieces = jnp.where(row == 0, high, jnp.where(row == 1, middle, jnp.where(row == 2, low, 0.0)))
    keep_ref[rows:, :] = pieces.astype(jnp.bfloat16)
    copies[4].wait()
    for ref, first in ((a_ref, 0), (b_ref, half)):
        for k in range(slabs):
            part, lanes = slice(first, first + half), slice(k * LANES, (k + 1) * LANES)
            ref[k * half : (k + 1) * half, :] = normed[part, lanes]
            ref[(slabs + k) * half : (slabs + k + 1) * half, :] = grad_s[part, lanes]
        here = (token >= first) & (token < first + half)
        ref[2 * slabs * half :, :] = jnp.where(here, dense, 0.0).astype(jnp.bfloat16)


def pack(x, grad, gain, routes, gates, experts):
    rows, width = x.shape
    top = routes.shape[1]
    shape = pltpu.VMEM((width // LANES * rows + -(-experts // 16) * 16, LANES), jnp.bfloat16)
    args = (x, grad, gain, routes.T, gates.T)
    return pl.pallas_call(
        pack_kernel,
        out_shape=(shape, shape, pltpu.VMEM((rows + 16, width), jnp.bfloat16)),
        in_specs=[pl.BlockSpec(memory_space=pltpu.HBM)] * 5,
        out_specs=(pl.BlockSpec(memory_space=pltpu.VMEM),) * 3,
        scratch_shapes=[
            pltpu.VMEM((rows, width), jnp.bfloat16),
            pltpu.VMEM((1, width), jnp.float32),
            pltpu.VMEM((top, rows), jnp.int32),
            pltpu.VMEM((top, rows), jnp.bfloat16),
            pltpu.SemaphoreType.DMA((5,)),
        ],
        compiler_params=pltpu.CompilerParams(vmem_limit_bytes=VMEM),
        name="pack",
    )(*(pltpu.with_memory_space_constraint(value, pltpu.HBM) for value in args))


def hold_kernel(*refs):
    count = len(refs) // 2
    copies = [pltpu.make_async_copy(refs[i], refs[count + i], refs[-1].at[i]) for i in range(count)]
    for copy in copies:
        copy.start()
    for copy in copies:
        copy.wait()


def hold(*values):
    return pl.pallas_call(
        hold_kernel,
        out_shape=[pltpu.VMEM(value.shape, value.dtype) for value in values],
        in_specs=[pl.BlockSpec(memory_space=pltpu.HBM)] * len(values),
        out_specs=[pl.BlockSpec(memory_space=pltpu.VMEM)] * len(values),
        scratch_shapes=[pltpu.SemaphoreType.DMA((len(values),))],
        compiler_params=pltpu.CompilerParams(vmem_limit_bytes=1 << 20),
        name="hold",
    )(*(pltpu.with_memory_space_constraint(value, pltpu.HBM) for value in values))


def turn_kernel(up_hbm, down_hbm, up_ref, up_t_ref, down_t_ref, down_ref, sems):
    copies = [
        pltpu.make_async_copy(up_hbm, up_ref, sems.at[0]),
        pltpu.make_async_copy(down_hbm, down_ref, sems.at[1]),
    ]
    for copy in copies:
        copy.start()
    for copy, value, turned in zip(copies, (up_ref, down_ref), (up_t_ref, down_t_ref)):
        copy.wait()
        for first in range(0, value.shape[0], 256):
            turned[:, first : first + 256] = value[first : first + 256, :].T


def turn(up, down):
    whole = pl.BlockSpec(memory_space=pltpu.VMEM)
    return pl.pallas_call(
        turn_kernel,
        out_shape=[pltpu.VMEM(shape, up.dtype) for shape in (up.shape, up.shape[::-1], down.shape[::-1])],
        in_specs=[pl.BlockSpec(memory_space=pltpu.HBM)] * 2,
        out_specs=[whole] * 3,
        scratch_shapes=[pltpu.VMEM(down.shape, down.dtype), pltpu.SemaphoreType.DMA((2,))],
        compiler_params=pltpu.CompilerParams(vmem_limit_bytes=VMEM),
        name="turn",
    )(*(pltpu.with_memory_space_constraint(value, pltpu.HBM) for value in (up, down)))


def expert_kernel(me_ref, a_ref, b_ref, *refs):
    o_ref = refs[-1]
    rows, width = o_ref.shape
    half, slabs = rows // 2, width // LANES

    def features(first):
        return jnp.concatenate(
            [
                jnp.concatenate([ref[k * half : (k + 1) * half, :] for k in range(first, first + slabs)], axis=1)
                for ref in (a_ref, b_ref)
            ],
            axis=0,
        )

    normed, grad = features(0), features(slabs)
    dense = sum(ref[2 * slabs * half :, :].astype(jnp.float32) for ref in (a_ref, b_ref))
    expert = lax.broadcasted_iota(jnp.int32, dense.shape, 0)
    square = (rows, rows)
    on_line = lax.broadcasted_iota(jnp.int32, square, 0) == lax.broadcasted_iota(jnp.int32, square, 1)
    for i, (up_ref, up_t_ref, down_t_ref) in enumerate((refs[:3], refs[3:6])):
        before = jnp.dot(normed, up_ref[...], preferred_element_type=jnp.float32)
        d_hidden = jnp.dot(grad, down_t_ref[...], preferred_element_type=jnp.float32)
        sigmoid_of = jax.nn.sigmoid(before)
        d_before = (d_hidden * sigmoid_of * (1.0 + before * (1.0 - sigmoid_of))).astype(jnp.bfloat16)
        d_route = jnp.dot(d_before, up_t_ref[...], preferred_element_type=jnp.float32)
        named = jnp.sum(jnp.where(expert == me_ref[i], dense, 0.0), axis=0, keepdims=True)
        gate = jnp.sum(jnp.where(on_line, jnp.broadcast_to(named, square), 0.0), axis=-1, keepdims=True)
        part = d_route.astype(jnp.bfloat16).astype(jnp.float32) * gate
        if i == 0:
            o_ref[...] = part
        else:
            o_ref[...] += part


def expert_part(me, a, b, rows, weights):
    width, hidden = weights[0].shape
    whole = pl.BlockSpec(memory_space=pltpu.VMEM)
    return pl.pallas_call(
        expert_kernel,
        out_shape=jax.ShapeDtypeStruct((rows, width), jnp.float32),
        in_specs=[pl.BlockSpec(memory_space=pltpu.SMEM)] + [whole] * 8,
        out_specs=whole,
        compiler_params=pltpu.CompilerParams(vmem_limit_bytes=VMEM),
        cost_estimate=pl.CostEstimate(
            flops=12 * rows * width * hidden,
            transcendentals=2 * rows * hidden,
            bytes_accessed=8 * width * hidden + 8 * rows * width,
        ),
        name="expert_part",
    )(me, a, b, *weights)


def finish_kernel(keep_ref, g_ref, own_ref, a_ref, b_ref, o_ref):
    half = a_ref.shape[0]
    rows = 2 * half
    pieces = keep_ref[rows : rows + 16, :].astype(jnp.float32)
    gain = (pieces[0:1, :] + pieces[1:2, :]) + pieces[2:3, :]
    for ref, first in ((a_ref, 0), (b_ref, half)):
        part = slice(first, first + half)
        values = keep_ref[part, :].astype(jnp.float32)
        scaling = lax.rsqrt(jnp.mean(values * values, axis=-1, keepdims=True) + epsilon)
        d_normed = own_ref[part, :].astype(jnp.float32) + ref[...].astype(jnp.float32)
        weighted = gain * d_normed
        inner_mean = jnp.mean(values * weighted, axis=-1, keepdims=True)
        back = scaling * weighted - values * (scaling * scaling * scaling) * inner_mean
        o_ref[part, :] = (g_ref[part, :].astype(jnp.float32) + back).astype(jnp.bfloat16)


def finish(keep, grad, own, a, b):
    return pl.pallas_call(
        finish_kernel,
        out_shape=jax.ShapeDtypeStruct(grad.shape, jnp.bfloat16),
        compiler_params=pltpu.CompilerParams(vmem_limit_bytes=VMEM),
        name="finish",
    )(keep, grad, own, a, b)


def shards(bwd_input, out_grad, norm_gain, up_weight, down_weight, bwd_routes, bwd_gates):
    experts = lax.axis_size("expert")
    sections = lax.axis_size("pipe")
    chips = experts // 2
    ring = list(range(0, chips, 2)) + list(range(1, chips, 2))[::-1]

    def hop(value, by):
        moves = [(ring[i], ring[(i + by) % chips]) for i in range(chips)]
        return lax.ppermute(value, "expert", [(2 * a + c, 2 * b + c) for a, b in moves for c in (0, 1)])

    def last_hop(value, by):
        moves = [(ring[i], ring[(i + by) % chips]) for i in range(chips)]
        return lax.ppermute(
            value,
            ("pipe", "expert"),
            [
                (s * experts + 2 * a + c, (s - 1) % sections * experts + 2 * b + c)
                for s in range(sections)
                for a, b in moves
                for c in (0, 1)
            ],
        )

    def to_previous(value):
        return lax.ppermute(value, "pipe", [(s, (s - 1) % sections) for s in range(sections)])

    def swap(value):
        return lax.ppermute(value, "expert", [(e, e ^ 1) for e in range(experts)])

    x, grad = bwd_input[0], out_grad[0]
    u0, d0 = up_weight[0, 0], down_weight[0, 0]
    e = lax.axis_index("expert").astype(jnp.int32)
    me = jnp.stack([e, e ^ 1])

    half = grad.shape[0] // 2
    u1, d1 = swap(u0), swap(d0)
    a, b, keep = pack(x, grad, norm_gain, bwd_routes[0], bwd_gates[0], experts)
    a1, b1 = hop(a, 1), hop(b, -1)
    weights = (*turn(u0, d0), *turn(u1, d1))
    own = expert_part(me, a, b, 2 * half, weights).astype(jnp.bfloat16)
    own_out, keep_out, grad_out = to_previous(own), to_previous(keep), to_previous(grad)
    early = {3: own, 2: keep_out, 5: grad_out, 6: own_out}
    sum_a = sum_b = None
    for step in range(1, chips):
        a, b = a1, b1
        if step in early:
            a, b, early[step] = lax.optimization_barrier((a, b, early[step]))
        if step < chips - 1:
            a1, b1 = hop(a, 1), hop(b, -1)
        part = expert_part(me, a, b, 2 * half, weights)
        part_a, part_b = part[:half], part[half:]
        if step > 1:
            part_a = part_a + sum_a.astype(jnp.float32)
            part_b = part_b + sum_b.astype(jnp.float32)
        send_a, send_b = part_a.astype(jnp.bfloat16), part_b.astype(jnp.bfloat16)
        if step == chips - 2:
            a1, send_a = lax.optimization_barrier((a1, send_a))
            b1, send_b = lax.optimization_barrier((b1, send_b))
        move = hop if step < chips - 1 else last_hop
        sum_a, sum_b = move(send_a, 1), move(send_b, -1)
    held = hold(keep_out, grad_out, own_out)
    return finish(*held, sum_a, sum_b)[None]


def solution(mesh):
    return jax.shard_map(
        shards,
        mesh=mesh,
        in_specs=(
            P("pipe", "expert", None),
            P("pipe", "expert", None),
            P("pipe", None),
            P("pipe", "expert", None, None),
            P("pipe", "expert", None, None),
            P("pipe", "expert", None),
            P("pipe", "expert", None),
        ),
        out_specs=P("pipe", "expert", None),
        check_vma=False,
    )
```

```python
import jax
import jax.numpy as jnp
from jax import lax
from jax.experimental import pallas as pl
from jax.experimental.pallas import tpu as pltpu
from jax.sharding import PartitionSpec as P

epsilon = 1e-06
LANES = 128
VMEM = 16 << 20


def pack_kernel(x_hbm, grad_hbm, gain_hbm, routes_hbm, gates_hbm, a_ref, b_ref, keep_ref, grad_s, gain_s, routes_s, gates_s, sems):
    rows, width = x_hbm.shape
    half, slabs = rows // 2, width // LANES
    parts = (slice(0, half), slice(half, rows))
    pairs = [(gain_hbm, gain_s)]
    pairs += [(x_hbm.at[part], keep_ref.at[part]) for part in parts]
    pairs += [(routes_hbm, routes_s), (gates_hbm, gates_s)]
    pairs += [(grad_hbm.at[part], grad_s.at[part]) for part in parts]
    copies = [pltpu.make_async_copy(hbm, vmem, sems.at[i]) for i, (hbm, vmem) in enumerate(pairs)]
    for copy in copies:
        copy.start()
    copies[0].wait()
    gain = gain_s[...]
    high = gain.astype(jnp.bfloat16).astype(jnp.float32)
    middle = (gain - high).astype(jnp.bfloat16).astype(jnp.float32)
    low = gain - high - middle
    row = lax.broadcasted_iota(jnp.int32, (keep_ref.shape[0] - rows, width), 0)
    pieces = jnp.where(row == 0, high, jnp.where(row == 1, middle, jnp.where(row == 2, low, 0.0)))
    keep_ref[rows:, :] = pieces.astype(jnp.bfloat16)
    for ref, part, copy in zip((a_ref, b_ref), parts, copies[1:3]):
        copy.wait()
        values = keep_ref[part, :].astype(jnp.float32)
        scaling = lax.rsqrt(jnp.mean(values * values, axis=-1, keepdims=True) + epsilon)
        normed = (values * scaling * gain).astype(jnp.bfloat16)
        for k in range(slabs):
            ref[k * half : (k + 1) * half, :] = normed[:, k * LANES : (k + 1) * LANES]
    copies[3].wait()
    copies[4].wait()
    shape = (a_ref.shape[0] - 2 * slabs * half, rows)
    expert = lax.broadcasted_iota(jnp.int32, shape, 0)
    token = lax.broadcasted_iota(jnp.int32, shape, 1)
    dense = jnp.zeros(shape, jnp.float32)
    routes, gates = routes_s[...], gates_s[...].astype(jnp.float32)
    for k in range(routes.shape[0]):
        dense = dense + jnp.where(expert == routes[k : k + 1, :], gates[k : k + 1, :], 0.0)
    for ref, part, copy in zip((a_ref, b_ref), parts, copies[5:]):
        copy.wait()
        for k in range(slabs):
            ref[(slabs + k) * half : (slabs + k + 1) * half, :] = grad_s[part, k * LANES : (k + 1) * LANES]
        here = (token >= part.start) & (token < part.stop)
        ref[2 * slabs * half :, :] = jnp.where(here, dense, 0.0).astype(jnp.bfloat16)


def pack(x, grad, gain, routes, gates, experts):
    rows, width = x.shape
    top = routes.shape[1]
    shape = pltpu.VMEM((width // LANES * rows + -(-experts // 16) * 16, LANES), jnp.bfloat16)
    args = (x, grad, gain, routes.T, gates.T)
    return pl.pallas_call(
        pack_kernel,
        out_shape=(shape, shape, pltpu.VMEM((rows + 16, width), jnp.bfloat16)),
        in_specs=[pl.BlockSpec(memory_space=pltpu.HBM)] * 5,
        out_specs=(pl.BlockSpec(memory_space=pltpu.VMEM),) * 3,
        scratch_shapes=[
            pltpu.VMEM((rows, width), jnp.bfloat16),
            pltpu.VMEM((1, width), jnp.float32),
            pltpu.VMEM((top, rows), jnp.int32),
            pltpu.VMEM((top, rows), jnp.bfloat16),
            pltpu.SemaphoreType.DMA((7,)),
        ],
        compiler_params=pltpu.CompilerParams(vmem_limit_bytes=VMEM),
        name="pack",
    )(*(pltpu.with_memory_space_constraint(value, pltpu.HBM) for value in args))


def hold_kernel(*refs):
    count = len(refs) // 2
    copies = [pltpu.make_async_copy(refs[i], refs[count + i], refs[-1].at[i]) for i in range(count)]
    for copy in copies:
        copy.start()
    for copy in copies:
        copy.wait()


def hold(*values):
    return pl.pallas_call(
        hold_kernel,
        out_shape=[pltpu.VMEM(value.shape, value.dtype) for value in values],
        in_specs=[pl.BlockSpec(memory_space=pltpu.HBM)] * len(values),
        out_specs=[pl.BlockSpec(memory_space=pltpu.VMEM)] * len(values),
        scratch_shapes=[pltpu.SemaphoreType.DMA((len(values),))],
        compiler_params=pltpu.CompilerParams(vmem_limit_bytes=1 << 20),
        name="hold",
    )(*(pltpu.with_memory_space_constraint(value, pltpu.HBM) for value in values))


def turn_kernel(up_hbm, down_hbm, up_ref, up_t_ref, down_t_ref, down_ref, sems):
    copies = [
        pltpu.make_async_copy(up_hbm, up_ref, sems.at[0]),
        pltpu.make_async_copy(down_hbm, down_ref, sems.at[1]),
    ]
    for copy in copies:
        copy.start()
    for copy, value, turned in zip(copies, (up_ref, down_ref), (up_t_ref, down_t_ref)):
        copy.wait()
        for first in range(0, value.shape[0], 256):
            turned[:, first : first + 256] = value[first : first + 256, :].T


def turn(up, down):
    whole = pl.BlockSpec(memory_space=pltpu.VMEM)
    return pl.pallas_call(
        turn_kernel,
        out_shape=[pltpu.VMEM(shape, up.dtype) for shape in (up.shape, up.shape[::-1], down.shape[::-1])],
        in_specs=[pl.BlockSpec(memory_space=pltpu.HBM)] * 2,
        out_specs=[whole] * 3,
        scratch_shapes=[pltpu.VMEM(down.shape, down.dtype), pltpu.SemaphoreType.DMA((2,))],
        compiler_params=pltpu.CompilerParams(vmem_limit_bytes=VMEM),
        name="turn",
    )(*(pltpu.with_memory_space_constraint(value, pltpu.HBM) for value in (up, down)))


def expert_kernel(me_ref, a_ref, b_ref, *refs):
    o_ref = refs[-1]
    rows, width = o_ref.shape
    half, slabs = rows // 2, width // LANES

    def features(first):
        return jnp.concatenate(
            [
                jnp.concatenate([ref[k * half : (k + 1) * half, :] for k in range(first, first + slabs)], axis=1)
                for ref in (a_ref, b_ref)
            ],
            axis=0,
        )

    normed, grad = features(0), features(slabs)
    dense = sum(ref[2 * slabs * half :, :].astype(jnp.float32) for ref in (a_ref, b_ref))
    expert = lax.broadcasted_iota(jnp.int32, dense.shape, 0)
    square = (rows, rows)
    on_line = lax.broadcasted_iota(jnp.int32, square, 0) == lax.broadcasted_iota(jnp.int32, square, 1)
    for i, (up_ref, up_t_ref, down_t_ref) in enumerate((refs[:3], refs[3:6])):
        before = jnp.dot(normed, up_ref[...], preferred_element_type=jnp.float32)
        d_hidden = jnp.dot(grad, down_t_ref[...], preferred_element_type=jnp.float32)
        sigmoid_of = jax.nn.sigmoid(before)
        d_before = (d_hidden * sigmoid_of * (1.0 + before * (1.0 - sigmoid_of))).astype(jnp.bfloat16)
        d_route = jnp.dot(d_before, up_t_ref[...], preferred_element_type=jnp.float32)
        named = jnp.sum(jnp.where(expert == me_ref[i], dense, 0.0), axis=0, keepdims=True)
        gate = jnp.sum(jnp.where(on_line, jnp.broadcast_to(named, square), 0.0), axis=-1, keepdims=True)
        part = d_route.astype(jnp.bfloat16).astype(jnp.float32) * gate
        if i == 0:
            o_ref[...] = part
        else:
            o_ref[...] += part


def expert_part(me, a, b, rows, weights):
    width, hidden = weights[0].shape
    whole = pl.BlockSpec(memory_space=pltpu.VMEM)
    return pl.pallas_call(
        expert_kernel,
        out_shape=jax.ShapeDtypeStruct((rows, width), jnp.float32),
        in_specs=[pl.BlockSpec(memory_space=pltpu.SMEM)] + [whole] * 8,
        out_specs=whole,
        compiler_params=pltpu.CompilerParams(vmem_limit_bytes=VMEM),
        cost_estimate=pl.CostEstimate(
            flops=12 * rows * width * hidden,
            transcendentals=2 * rows * hidden,
            bytes_accessed=8 * width * hidden + 8 * rows * width,
        ),
        name="expert_part",
    )(me, a, b, *weights)


def settle_kernel(keep_hbm, g_hbm, own_hbm, base_ref, x_ref, rows_ref, keep_s, g_s, own_s, sems):
    copies = [
        pltpu.make_async_copy(hbm, vmem, sems.at[i])
        for i, (hbm, vmem) in enumerate(((keep_hbm, keep_s), (own_hbm, own_s), (g_hbm, g_s)))
    ]
    for copy in copies:
        copy.start()
    for copy in copies:
        copy.wait()
    rows = g_s.shape[0]
    pieces = keep_s[rows:, :].astype(jnp.float32)
    gain = (pieces[0:1, :] + pieces[1:2, :]) + pieces[2:3, :]
    values = keep_s[:rows, :].astype(jnp.float32)
    scaling = lax.rsqrt(jnp.mean(values * values, axis=-1, keepdims=True) + epsilon)
    weighted = gain * own_s[...].astype(jnp.float32)
    inner_mean = jnp.mean(values * weighted, axis=-1, keepdims=True)
    back = scaling * weighted - values * (scaling * scaling * scaling) * inner_mean
    base_ref[...] = g_s[...].astype(jnp.float32) + back
    x_ref[...] = values
    rows_ref[0:8, :] = jnp.broadcast_to(gain, (8, gain.shape[1]))
    rows_ref[8:, :LANES] = jnp.broadcast_to(scaling, (rows, LANES))


def settle(keep, grad, own):
    rows, width = grad.shape
    whole = pl.BlockSpec(memory_space=pltpu.VMEM)
    full = pltpu.VMEM((rows, width), jnp.float32)
    return pl.pallas_call(
        settle_kernel,
        out_shape=[full, full, pltpu.VMEM((rows + 8, width), jnp.float32)],
        in_specs=[pl.BlockSpec(memory_space=pltpu.HBM)] * 3,
        out_specs=[whole] * 3,
        scratch_shapes=[pltpu.VMEM(value.shape, value.dtype) for value in (keep, grad, own)]
        + [pltpu.SemaphoreType.DMA((3,))],
        compiler_params=pltpu.CompilerParams(vmem_limit_bytes=VMEM),
        name="settle",
    )(*(pltpu.with_memory_space_constraint(value, pltpu.HBM) for value in (keep, grad, own)))


def finish_kernel(base_ref, x_ref, rows_ref, a_ref, b_ref, o_ref):
    half = a_ref.shape[0]
    gain = rows_ref[0:1, :]
    for ref, first in ((a_ref, 0), (b_ref, half)):
        part = slice(first, first + half)
        scaling = rows_ref[8 + first : 8 + first + half, 0:1]
        weighted = gain * ref[...].astype(jnp.float32)
        values = x_ref[part, :]
        inner_mean = jnp.mean(values * weighted, axis=-1, keepdims=True)
        back = scaling * weighted - values * ((scaling * scaling * scaling) * inner_mean)
        o_ref[part, :] = (base_ref[part, :] + back).astype(jnp.bfloat16)


def finish(base, x, rows, a, b):
    return pl.pallas_call(
        finish_kernel,
        out_shape=jax.ShapeDtypeStruct(x.shape, jnp.bfloat16),
        compiler_params=pltpu.CompilerParams(vmem_limit_bytes=VMEM),
        name="finish",
    )(base, x, rows, a, b)


def shards(bwd_input, out_grad, norm_gain, up_weight, down_weight, bwd_routes, bwd_gates):
    experts = lax.axis_size("expert")
    sections = lax.axis_size("pipe")
    chips = experts // 2
    ring = list(range(0, chips, 2)) + list(range(1, chips, 2))[::-1]

    def hop(value, by):
        moves = [(ring[i], ring[(i + by) % chips]) for i in range(chips)]
        return lax.ppermute(value, "expert", [(2 * a + c, 2 * b + c) for a, b in moves for c in (0, 1)])

    def last_hop(value, by):
        moves = [(ring[i], ring[(i + by) % chips]) for i in range(chips)]
        return lax.ppermute(
            value,
            ("pipe", "expert"),
            [
                (s * experts + 2 * a + c, (s - 1) % sections * experts + 2 * b + c)
                for s in range(sections)
                for a, b in moves
                for c in (0, 1)
            ],
        )

    def to_previous(value):
        return lax.ppermute(value, "pipe", [(s, (s - 1) % sections) for s in range(sections)])

    def swap(value):
        return lax.ppermute(value, "expert", [(e, e ^ 1) for e in range(experts)])

    x, grad = bwd_input[0], out_grad[0]
    u0, d0 = up_weight[0, 0], down_weight[0, 0]
    e = lax.axis_index("expert").astype(jnp.int32)
    me = jnp.stack([e, e ^ 1])

    half = grad.shape[0] // 2
    u1, d1 = swap(u0), swap(d0)
    a, b, keep = pack(x, grad, norm_gain, bwd_routes[0], bwd_gates[0], experts)
    a1, b1 = hop(a, 1), hop(b, -1)
    weights = (*turn(u0, d0), *turn(u1, d1))
    own = expert_part(me, a, b, 2 * half, weights).astype(jnp.bfloat16)
    own_out, keep_out, grad_out = to_previous(own), to_previous(keep), to_previous(grad)
    early = {3: own, 2: keep_out, 5: grad_out, 6: own_out}
    sum_a = sum_b = None
    for step in range(1, chips):
        a, b = a1, b1
        if step in early:
            a, b, early[step] = lax.optimization_barrier((a, b, early[step]))
        if step < chips - 1:
            a1, b1 = hop(a, 1), hop(b, -1)
        part = expert_part(me, a, b, 2 * half, weights)
        part_a, part_b = part[:half], part[half:]
        if step > 1:
            part_a = part_a + sum_a.astype(jnp.float32)
            part_b = part_b + sum_b.astype(jnp.float32)
        send_a, send_b = part_a.astype(jnp.bfloat16), part_b.astype(jnp.bfloat16)
        if step == chips - 2:
            a1, send_a = lax.optimization_barrier((a1, send_a))
            b1, send_b = lax.optimization_barrier((b1, send_b))
        move = hop if step < chips - 1 else last_hop
        sum_a, sum_b = move(send_a, 1), move(send_b, -1)
    held = settle(keep_out, grad_out, own_out)
    return finish(*held, sum_a, sum_b)[None]


def solution(mesh):
    return jax.shard_map(
        shards,
        mesh=mesh,
        in_specs=(
            P("pipe", "expert", None),
            P("pipe", "expert", None),
            P("pipe", None),
            P("pipe", "expert", None, None),
            P("pipe", "expert", None, None),
            P("pipe", "expert", None),
            P("pipe", "expert", None),
        ),
        out_specs=P("pipe", "expert", None),
        check_vma=False,
    )
```

```python
import jax
import jax.numpy as jnp
from jax import lax
from jax.experimental import pallas as pl
from jax.experimental.pallas import tpu as pltpu
from jax.sharding import PartitionSpec as P

epsilon = 1e-06
LANES = 128
VMEM = 16 << 20


def pack_kernel(x_hbm, grad_hbm, gain_hbm, routes_hbm, gates_hbm, a_ref, b_ref, keep_ref, grad_s, gain_s, routes_s, gates_s, sems):
    rows, width = x_hbm.shape
    half, slabs = rows // 2, width // LANES
    parts = (slice(0, half), slice(half, rows))
    pairs = [(gain_hbm, gain_s)]
    pairs += [(x_hbm.at[part], keep_ref.at[part]) for part in parts]
    pairs += [(routes_hbm, routes_s), (gates_hbm, gates_s)]
    pairs += [(grad_hbm.at[part], grad_s.at[part]) for part in parts]
    copies = [pltpu.make_async_copy(hbm, vmem, sems.at[i]) for i, (hbm, vmem) in enumerate(pairs)]
    for copy in copies:
        copy.start()
    copies[0].wait()
    gain = gain_s[...]
    high = gain.astype(jnp.bfloat16).astype(jnp.float32)
    middle = (gain - high).astype(jnp.bfloat16).astype(jnp.float32)
    low = gain - high - middle
    row = lax.broadcasted_iota(jnp.int32, (keep_ref.shape[0] - rows, width), 0)
    pieces = jnp.where(row == 0, high, jnp.where(row == 1, middle, jnp.where(row == 2, low, 0.0)))
    keep_ref[rows:, :] = pieces.astype(jnp.bfloat16)
    for ref, part, copy in zip((a_ref, b_ref), parts, copies[1:3]):
        copy.wait()
        values = keep_ref[part, :].astype(jnp.float32)
        scaling = lax.rsqrt(jnp.mean(values * values, axis=-1, keepdims=True) + epsilon)
        normed = (values * scaling * gain).astype(jnp.bfloat16)
        for k in range(slabs):
            ref[k * half : (k + 1) * half, :] = normed[:, k * LANES : (k + 1) * LANES]
    copies[3].wait()
    copies[4].wait()
    shape = (a_ref.shape[0] - 2 * slabs * half, rows)
    expert = lax.broadcasted_iota(jnp.int32, shape, 0)
    token = lax.broadcasted_iota(jnp.int32, shape, 1)
    dense = jnp.zeros(shape, jnp.float32)
    routes, gates = routes_s[...], gates_s[...].astype(jnp.float32)
    for k in range(routes.shape[0]):
        dense = dense + jnp.where(expert == routes[k : k + 1, :], gates[k : k + 1, :], 0.0)
    for ref, part, copy in zip((a_ref, b_ref), parts, copies[5:]):
        copy.wait()
        for k in range(slabs):
            ref[(slabs + k) * half : (slabs + k + 1) * half, :] = grad_s[part, k * LANES : (k + 1) * LANES]
        here = (token >= part.start) & (token < part.stop)
        ref[2 * slabs * half :, :] = jnp.where(here, dense, 0.0).astype(jnp.bfloat16)


def pack(x, grad, gain, routes, gates, experts):
    rows, width = x.shape
    top = routes.shape[1]
    shape = pltpu.VMEM((width // LANES * rows + -(-experts // 16) * 16, LANES), jnp.bfloat16)
    args = (x, grad, gain, routes.T, gates.T)
    return pl.pallas_call(
        pack_kernel,
        out_shape=(shape, shape, pltpu.VMEM((rows + 16, width), jnp.bfloat16)),
        in_specs=[pl.BlockSpec(memory_space=pltpu.HBM)] * 5,
        out_specs=(pl.BlockSpec(memory_space=pltpu.VMEM),) * 3,
        scratch_shapes=[
            pltpu.VMEM((rows, width), jnp.bfloat16),
            pltpu.VMEM((1, width), jnp.float32),
            pltpu.VMEM((top, rows), jnp.int32),
            pltpu.VMEM((top, rows), jnp.bfloat16),
            pltpu.SemaphoreType.DMA((7,)),
        ],
        compiler_params=pltpu.CompilerParams(vmem_limit_bytes=VMEM),
        name="pack",
    )(*(pltpu.with_memory_space_constraint(value, pltpu.HBM) for value in args))


def hold_kernel(*refs):
    count = len(refs) // 2
    copies = [pltpu.make_async_copy(refs[i], refs[count + i], refs[-1].at[i]) for i in range(count)]
    for copy in copies:
        copy.start()
    for copy in copies:
        copy.wait()


def hold(*values):
    return pl.pallas_call(
        hold_kernel,
        out_shape=[pltpu.VMEM(value.shape, value.dtype) for value in values],
        in_specs=[pl.BlockSpec(memory_space=pltpu.HBM)] * len(values),
        out_specs=[pl.BlockSpec(memory_space=pltpu.VMEM)] * len(values),
        scratch_shapes=[pltpu.SemaphoreType.DMA((len(values),))],
        compiler_params=pltpu.CompilerParams(vmem_limit_bytes=1 << 20),
        name="hold",
    )(*(pltpu.with_memory_space_constraint(value, pltpu.HBM) for value in values))


def turn_kernel(up_hbm, down_hbm, up_ref, up_t_ref, down_t_ref, down_ref, sems):
    copies = [
        pltpu.make_async_copy(up_hbm, up_ref, sems.at[0]),
        pltpu.make_async_copy(down_hbm, down_ref, sems.at[1]),
    ]
    for copy in copies:
        copy.start()
    for copy, value, turned in zip(copies, (up_ref, down_ref), (up_t_ref, down_t_ref)):
        copy.wait()
        for first in range(0, value.shape[0], 256):
            turned[:, first : first + 256] = value[first : first + 256, :].T


def turn(up, down):
    whole = pl.BlockSpec(memory_space=pltpu.VMEM)
    return pl.pallas_call(
        turn_kernel,
        out_shape=[pltpu.VMEM(shape, up.dtype) for shape in (up.shape, up.shape[::-1], down.shape[::-1])],
        in_specs=[pl.BlockSpec(memory_space=pltpu.HBM)] * 2,
        out_specs=[whole] * 3,
        scratch_shapes=[pltpu.VMEM(down.shape, down.dtype), pltpu.SemaphoreType.DMA((2,))],
        compiler_params=pltpu.CompilerParams(vmem_limit_bytes=VMEM),
        name="turn",
    )(*(pltpu.with_memory_space_constraint(value, pltpu.HBM) for value in (up, down)))


def expert_kernel(me_ref, a_ref, b_ref, *refs):
    o_ref = refs[-1]
    rows, width = o_ref.shape
    half, slabs = rows // 2, width // LANES

    def features(first):
        return jnp.concatenate(
            [
                jnp.concatenate([ref[k * half : (k + 1) * half, :] for k in range(first, first + slabs)], axis=1)
                for ref in (a_ref, b_ref)
            ],
            axis=0,
        )

    normed, grad = features(0), features(slabs)
    dense = sum(ref[2 * slabs * half :, :].astype(jnp.float32) for ref in (a_ref, b_ref))
    expert = lax.broadcasted_iota(jnp.int32, dense.shape, 0)
    square = (rows, rows)
    on_line = lax.broadcasted_iota(jnp.int32, square, 0) == lax.broadcasted_iota(jnp.int32, square, 1)
    for i, (up_ref, up_t_ref, down_t_ref) in enumerate((refs[:3], refs[3:6])):
        before = jnp.dot(normed, up_ref[...], preferred_element_type=jnp.float32)
        d_hidden = jnp.dot(grad, down_t_ref[...], preferred_element_type=jnp.float32)
        sigmoid_of = jax.nn.sigmoid(before)
        d_before = (d_hidden * sigmoid_of * (1.0 + before * (1.0 - sigmoid_of))).astype(jnp.bfloat16)
        d_route = jnp.dot(d_before, up_t_ref[...], preferred_element_type=jnp.float32)
        named = jnp.sum(jnp.where(expert == me_ref[i], dense, 0.0), axis=0, keepdims=True)
        gate = jnp.sum(jnp.where(on_line, jnp.broadcast_to(named, square), 0.0), axis=-1, keepdims=True)
        part = d_route.astype(jnp.bfloat16).astype(jnp.float32) * gate
        if i == 0:
            o_ref[...] = part
        else:
            o_ref[...] += part


def expert_part(me, a, b, rows, weights):
    width, hidden = weights[0].shape
    whole = pl.BlockSpec(memory_space=pltpu.VMEM)
    return pl.pallas_call(
        expert_kernel,
        out_shape=jax.ShapeDtypeStruct((rows, width), jnp.float32),
        in_specs=[pl.BlockSpec(memory_space=pltpu.SMEM)] + [whole] * 8,
        out_specs=whole,
        compiler_params=pltpu.CompilerParams(vmem_limit_bytes=VMEM),
        cost_estimate=pl.CostEstimate(
            flops=12 * rows * width * hidden,
            transcendentals=2 * rows * hidden,
            bytes_accessed=8 * width * hidden + 8 * rows * width,
        ),
        name="expert_part",
    )(me, a, b, *weights)


def settle_kernel(keep_hbm, g_hbm, own_hbm, base_ref, x_ref, rows_ref, keep_s, g_s, own_s, sems):
    copies = [
        pltpu.make_async_copy(hbm, vmem, sems.at[i])
        for i, (hbm, vmem) in enumerate(((keep_hbm, keep_s), (own_hbm, own_s), (g_hbm, g_s)))
    ]
    for copy in copies:
        copy.start()
    for copy in copies:
        copy.wait()
    rows = g_s.shape[0]
    pieces = keep_s[rows:, :].astype(jnp.float32)
    gain = (pieces[0:1, :] + pieces[1:2, :]) + pieces[2:3, :]
    values = keep_s[:rows, :].astype(jnp.float32)
    scaling = lax.rsqrt(jnp.mean(values * values, axis=-1, keepdims=True) + epsilon)
    weighted = gain * own_s[...].astype(jnp.float32)
    inner_mean = jnp.mean(values * weighted, axis=-1, keepdims=True)
    back = scaling * weighted - values * (scaling * scaling * scaling) * inner_mean
    base_ref[...] = g_s[...].astype(jnp.float32) + back
    x_ref[...] = values
    rows_ref[0:8, :] = jnp.broadcast_to(gain, (8, gain.shape[1]))
    rows_ref[8:, :LANES] = jnp.broadcast_to(scaling, (rows, LANES))


def settle(keep, grad, own):
    rows, width = grad.shape
    whole = pl.BlockSpec(memory_space=pltpu.VMEM)
    full = pltpu.VMEM((rows, width), jnp.float32)
    return pl.pallas_call(
        settle_kernel,
        out_shape=[full, full, pltpu.VMEM((rows + 8, width), jnp.float32)],
        in_specs=[pl.BlockSpec(memory_space=pltpu.HBM)] * 3,
        out_specs=[whole] * 3,
        scratch_shapes=[pltpu.VMEM(value.shape, value.dtype) for value in (keep, grad, own)]
        + [pltpu.SemaphoreType.DMA((3,))],
        compiler_params=pltpu.CompilerParams(vmem_limit_bytes=VMEM),
        name="settle",
    )(*(pltpu.with_memory_space_constraint(value, pltpu.HBM) for value in (keep, grad, own)))


def finish_kernel(base_ref, x_ref, rows_ref, a_ref, b_ref, o_ref):
    half = a_ref.shape[0]
    gain = rows_ref[0:1, :]
    for ref, first in ((a_ref, 0), (b_ref, half)):
        part = slice(first, first + half)
        scaling = rows_ref[8 + first : 8 + first + half, 0:1]
        weighted = gain * ref[...].astype(jnp.float32)
        values = x_ref[part, :]
        inner_mean = jnp.mean(values * weighted, axis=-1, keepdims=True)
        back = scaling * weighted - values * ((scaling * scaling * scaling) * inner_mean)
        o_ref[part, :] = (base_ref[part, :] + back).astype(jnp.bfloat16)


def finish(base, x, rows, a, b):
    return pl.pallas_call(
        finish_kernel,
        out_shape=jax.ShapeDtypeStruct(x.shape, jnp.bfloat16),
        compiler_params=pltpu.CompilerParams(vmem_limit_bytes=VMEM),
        name="finish",
    )(base, x, rows, a, b)


def shards(bwd_input, out_grad, norm_gain, up_weight, down_weight, bwd_routes, bwd_gates):
    experts = lax.axis_size("expert")
    sections = lax.axis_size("pipe")
    chips = experts // 2
    ring = list(range(0, chips, 2)) + list(range(1, chips, 2))[::-1]

    def hop(value, by):
        moves = [(ring[i], ring[(i + by) % chips]) for i in range(chips)]
        return lax.ppermute(value, "expert", [(2 * a + c, 2 * b + c) for a, b in moves for c in (0, 1)])

    def last_hop(value, by):
        moves = [(ring[i], ring[(i + by) % chips]) for i in range(chips)]
        return lax.ppermute(
            value,
            ("pipe", "expert"),
            [
                (s * experts + 2 * a + c, (s - 1) % sections * experts + 2 * b + c)
                for s in range(sections)
                for a, b in moves
                for c in (0, 1)
            ],
        )

    def to_previous(value):
        return lax.ppermute(value, "pipe", [(s, (s - 1) % sections) for s in range(sections)])

    def swap(value):
        return lax.ppermute(value, "expert", [(e, e ^ 1) for e in range(experts)])

    x, grad = bwd_input[0], out_grad[0]
    u0, d0 = up_weight[0, 0], down_weight[0, 0]
    e = lax.axis_index("expert").astype(jnp.int32)
    me = jnp.stack([e, e ^ 1])

    half = grad.shape[0] // 2
    u1, d1 = swap(u0), swap(d0)
    a, b, keep = pack(x, grad, norm_gain, bwd_routes[0], bwd_gates[0], experts)
    a1, b1 = hop(a, 1), hop(b, -1)
    weights = (*turn(u0, d0), *turn(u1, d1))
    own = expert_part(me, a, b, 2 * half, weights).astype(jnp.bfloat16)
    own_out, keep_out, grad_out = to_previous(own), to_previous(keep), to_previous(grad)
    early = {3: own, 2: keep_out, 5: grad_out, 6: own_out}
    sum_a = sum_b = None
    for step in range(1, chips):
        a, b = a1, b1
        if step in early:
            a, b, early[step] = lax.optimization_barrier((a, b, early[step]))
        if step < chips - 1:
            a1, b1 = hop(a, 1), hop(b, -1)
        part = expert_part(me, a, b, 2 * half, weights)
        part_a, part_b = part[:half], part[half:]
        if step > 1:
            part_a = part_a + sum_a.astype(jnp.float32)
            part_b = part_b + sum_b.astype(jnp.float32)
        send_a, send_b = part_a.astype(jnp.bfloat16), part_b.astype(jnp.bfloat16)
        move = hop if step < chips - 1 else last_hop
        sum_a, sum_b = move(send_a, 1), move(send_b, -1)
    held = settle(keep_out, grad_out, own_out)
    return finish(*held, sum_a, sum_b)[None]


def solution(mesh):
    return jax.shard_map(
        shards,
        mesh=mesh,
        in_specs=(
            P("pipe", "expert", None),
            P("pipe", "expert", None),
            P("pipe", None),
            P("pipe", "expert", None, None),
            P("pipe", "expert", None, None),
            P("pipe", "expert", None),
            P("pipe", "expert", None),
        ),
        out_specs=P("pipe", "expert", None),
        check_vma=False,
    )
```

```python
import jax
import jax.numpy as jnp
from jax import lax
from jax.experimental import pallas as pl
from jax.experimental.pallas import tpu as pltpu
from jax.sharding import PartitionSpec as P

epsilon = 1e-06
LANES = 128
VMEM = 16 << 20


def pack_kernel(x_hbm, grad_hbm, gain_hbm, routes_hbm, gates_hbm, a_ref, b_ref, keep_ref, grad_s, gain_s, routes_s, gates_s, sems):
    rows, width = x_hbm.shape
    half, slabs = rows // 2, width // LANES
    parts = (slice(0, half), slice(half, rows))
    pairs = [(gain_hbm, gain_s)]
    pairs += [(x_hbm.at[part], keep_ref.at[part]) for part in parts]
    pairs += [(routes_hbm, routes_s), (gates_hbm, gates_s)]
    pairs += [(grad_hbm.at[part], grad_s.at[part]) for part in parts]
    copies = [pltpu.make_async_copy(hbm, vmem, sems.at[i]) for i, (hbm, vmem) in enumerate(pairs)]
    for copy in copies:
        copy.start()
    copies[0].wait()
    gain = gain_s[...]
    high = gain.astype(jnp.bfloat16).astype(jnp.float32)
    middle = (gain - high).astype(jnp.bfloat16).astype(jnp.float32)
    low = gain - high - middle
    row = lax.broadcasted_iota(jnp.int32, (keep_ref.shape[0] - rows, width), 0)
    pieces = jnp.where(row == 0, high, jnp.where(row == 1, middle, jnp.where(row == 2, low, 0.0)))
    keep_ref[rows:, :] = pieces.astype(jnp.bfloat16)
    for ref, part, copy in zip((a_ref, b_ref), parts, copies[1:3]):
        copy.wait()
        values = keep_ref[part, :].astype(jnp.float32)
        scaling = lax.rsqrt(jnp.mean(values * values, axis=-1, keepdims=True) + epsilon)
        normed = (values * scaling * gain).astype(jnp.bfloat16)
        for k in range(slabs):
            ref[k * half : (k + 1) * half, :] = normed[:, k * LANES : (k + 1) * LANES]
    copies[3].wait()
    copies[4].wait()
    shape = (a_ref.shape[0] - 2 * slabs * half, rows)
    expert = lax.broadcasted_iota(jnp.int32, shape, 0)
    token = lax.broadcasted_iota(jnp.int32, shape, 1)
    dense = jnp.zeros(shape, jnp.float32)
    routes, gates = routes_s[...], gates_s[...].astype(jnp.float32)
    for k in range(routes.shape[0]):
        dense = dense + jnp.where(expert == routes[k : k + 1, :], gates[k : k + 1, :], 0.0)
    for ref, part, copy in zip((a_ref, b_ref), parts, copies[5:]):
        copy.wait()
        for k in range(slabs):
            ref[(slabs + k) * half : (slabs + k + 1) * half, :] = grad_s[part, k * LANES : (k + 1) * LANES]
        here = (token >= part.start) & (token < part.stop)
        ref[2 * slabs * half :, :] = jnp.where(here, dense, 0.0).astype(jnp.bfloat16)


def pack(x, grad, gain, routes, gates, experts):
    rows, width = x.shape
    top = routes.shape[1]
    shape = pltpu.VMEM((width // LANES * rows + -(-experts // 16) * 16, LANES), jnp.bfloat16)
    args = (x, grad, gain, routes.T, gates.T)
    return pl.pallas_call(
        pack_kernel,
        out_shape=(shape, shape, pltpu.VMEM((rows + 16, width), jnp.bfloat16)),
        in_specs=[pl.BlockSpec(memory_space=pltpu.HBM)] * 5,
        out_specs=(pl.BlockSpec(memory_space=pltpu.VMEM),) * 3,
        scratch_shapes=[
            pltpu.VMEM((rows, width), jnp.bfloat16),
            pltpu.VMEM((1, width), jnp.float32),
            pltpu.VMEM((top, rows), jnp.int32),
            pltpu.VMEM((top, rows), jnp.bfloat16),
            pltpu.SemaphoreType.DMA((7,)),
        ],
        compiler_params=pltpu.CompilerParams(vmem_limit_bytes=VMEM),
        name="pack",
    )(*(pltpu.with_memory_space_constraint(value, pltpu.HBM) for value in args))


def hold_kernel(*refs):
    count = len(refs) // 2
    copies = [pltpu.make_async_copy(refs[i], refs[count + i], refs[-1].at[i]) for i in range(count)]
    for copy in copies:
        copy.start()
    for copy in copies:
        copy.wait()


def hold(*values):
    return pl.pallas_call(
        hold_kernel,
        out_shape=[pltpu.VMEM(value.shape, value.dtype) for value in values],
        in_specs=[pl.BlockSpec(memory_space=pltpu.HBM)] * len(values),
        out_specs=[pl.BlockSpec(memory_space=pltpu.VMEM)] * len(values),
        scratch_shapes=[pltpu.SemaphoreType.DMA((len(values),))],
        compiler_params=pltpu.CompilerParams(vmem_limit_bytes=1 << 20),
        name="hold",
    )(*(pltpu.with_memory_space_constraint(value, pltpu.HBM) for value in values))


def turn_kernel(up_hbm, down_hbm, up_ref, up_t_ref, down_t_ref, down_ref, sems):
    copies = [
        pltpu.make_async_copy(up_hbm, up_ref, sems.at[0]),
        pltpu.make_async_copy(down_hbm, down_ref, sems.at[1]),
    ]
    for copy in copies:
        copy.start()
    for copy, value, turned in zip(copies, (up_ref, down_ref), (up_t_ref, down_t_ref)):
        copy.wait()
        for first in range(0, value.shape[0], 256):
            turned[:, first : first + 256] = value[first : first + 256, :].T


def turn(up, down):
    whole = pl.BlockSpec(memory_space=pltpu.VMEM)
    return pl.pallas_call(
        turn_kernel,
        out_shape=[pltpu.VMEM(shape, up.dtype) for shape in (up.shape, up.shape[::-1], down.shape[::-1])],
        in_specs=[pl.BlockSpec(memory_space=pltpu.HBM)] * 2,
        out_specs=[whole] * 3,
        scratch_shapes=[pltpu.VMEM(down.shape, down.dtype), pltpu.SemaphoreType.DMA((2,))],
        compiler_params=pltpu.CompilerParams(vmem_limit_bytes=VMEM),
        name="turn",
    )(*(pltpu.with_memory_space_constraint(value, pltpu.HBM) for value in (up, down)))


def expert_kernel(me_ref, a_ref, b_ref, *refs):
    o_ref = refs[-1]
    rows, width = o_ref.shape
    half, slabs = rows // 2, width // LANES

    def features(first):
        return jnp.concatenate(
            [
                jnp.concatenate([ref[k * half : (k + 1) * half, :] for k in range(first, first + slabs)], axis=1)
                for ref in (a_ref, b_ref)
            ],
            axis=0,
        )

    normed, grad = features(0), features(slabs)
    dense = sum(ref[2 * slabs * half :, :].astype(jnp.float32) for ref in (a_ref, b_ref))
    expert = lax.broadcasted_iota(jnp.int32, dense.shape, 0)
    square = (rows, rows)
    on_line = lax.broadcasted_iota(jnp.int32, square, 0) == lax.broadcasted_iota(jnp.int32, square, 1)
    for i, (up_ref, up_t_ref, down_t_ref) in enumerate((refs[:3], refs[3:6])):
        before = jnp.dot(normed, up_ref[...], preferred_element_type=jnp.float32)
        d_hidden = jnp.dot(grad, down_t_ref[...], preferred_element_type=jnp.float32)
        sigmoid_of = jax.nn.sigmoid(before)
        d_before = (d_hidden * sigmoid_of * (1.0 + before * (1.0 - sigmoid_of))).astype(jnp.bfloat16)
        d_route = jnp.dot(d_before, up_t_ref[...], preferred_element_type=jnp.float32)
        named = jnp.sum(jnp.where(expert == me_ref[i], dense, 0.0), axis=0, keepdims=True)
        gate = jnp.sum(jnp.where(on_line, jnp.broadcast_to(named, square), 0.0), axis=-1, keepdims=True)
        part = d_route.astype(jnp.bfloat16).astype(jnp.float32) * gate
        if i == 0:
            o_ref[...] = part
        else:
            o_ref[...] += part


def expert_part(me, a, b, rows, weights):
    width, hidden = weights[0].shape
    whole = pl.BlockSpec(memory_space=pltpu.VMEM)
    return pl.pallas_call(
        expert_kernel,
        out_shape=jax.ShapeDtypeStruct((rows, width), jnp.float32),
        in_specs=[pl.BlockSpec(memory_space=pltpu.SMEM)] + [whole] * 8,
        out_specs=whole,
        compiler_params=pltpu.CompilerParams(vmem_limit_bytes=VMEM),
        cost_estimate=pl.CostEstimate(
            flops=12 * rows * width * hidden,
            transcendentals=2 * rows * hidden,
            bytes_accessed=8 * width * hidden + 8 * rows * width,
        ),
        name="expert_part",
    )(me, a, b, *weights)


def settle_kernel(keep_hbm, g_hbm, own_hbm, base_ref, x_ref, rows_ref, keep_s, g_s, own_s, sems):
    copies = [
        pltpu.make_async_copy(hbm, vmem, sems.at[i])
        for i, (hbm, vmem) in enumerate(((keep_hbm, keep_s), (own_hbm, own_s), (g_hbm, g_s)))
    ]
    for copy in copies:
        copy.start()
    for copy in copies:
        copy.wait()
    rows = g_s.shape[0]
    pieces = keep_s[rows:, :].astype(jnp.float32)
    gain = (pieces[0:1, :] + pieces[1:2, :]) + pieces[2:3, :]
    values = keep_s[:rows, :].astype(jnp.float32)
    scaling = lax.rsqrt(jnp.mean(values * values, axis=-1, keepdims=True) + epsilon)
    weighted = gain * own_s[...].astype(jnp.float32)
    inner_mean = jnp.mean(values * weighted, axis=-1, keepdims=True)
    back = scaling * weighted - values * (scaling * scaling * scaling) * inner_mean
    base_ref[...] = g_s[...].astype(jnp.float32) + back
    x_ref[...] = values
    rows_ref[0:8, :] = jnp.broadcast_to(gain, (8, gain.shape[1]))
    rows_ref[8:, :LANES] = jnp.broadcast_to(scaling, (rows, LANES))


def settle(keep, grad, own):
    rows, width = grad.shape
    whole = pl.BlockSpec(memory_space=pltpu.VMEM)
    full = pltpu.VMEM((rows, width), jnp.float32)
    return pl.pallas_call(
        settle_kernel,
        out_shape=[full, full, pltpu.VMEM((rows + 8, width), jnp.float32)],
        in_specs=[pl.BlockSpec(memory_space=pltpu.HBM)] * 3,
        out_specs=[whole] * 3,
        scratch_shapes=[pltpu.VMEM(value.shape, value.dtype) for value in (keep, grad, own)]
        + [pltpu.SemaphoreType.DMA((3,))],
        compiler_params=pltpu.CompilerParams(vmem_limit_bytes=VMEM),
        name="settle",
    )(*(pltpu.with_memory_space_constraint(value, pltpu.HBM) for value in (keep, grad, own)))


def finish_kernel(base_ref, x_ref, rows_ref, a_ref, b_ref, o_ref):
    half = a_ref.shape[0]
    gain = rows_ref[0:1, :]
    for ref, first in ((a_ref, 0), (b_ref, half)):
        part = slice(first, first + half)
        scaling = rows_ref[8 + first : 8 + first + half, 0:1]
        weighted = gain * ref[...].astype(jnp.float32)
        values = x_ref[part, :]
        inner_mean = jnp.mean(values * weighted, axis=-1, keepdims=True)
        back = scaling * weighted - values * ((scaling * scaling * scaling) * inner_mean)
        o_ref[part, :] = (base_ref[part, :] + back).astype(jnp.bfloat16)


def finish(base, x, rows, a, b):
    return pl.pallas_call(
        finish_kernel,
        out_shape=jax.ShapeDtypeStruct(x.shape, jnp.bfloat16),
        compiler_params=pltpu.CompilerParams(vmem_limit_bytes=VMEM),
        name="finish",
    )(base, x, rows, a, b)


def shards(bwd_input, out_grad, norm_gain, up_weight, down_weight, bwd_routes, bwd_gates):
    experts = lax.axis_size("expert")
    sections = lax.axis_size("pipe")
    chips = experts // 2
    ring = list(range(0, chips, 2)) + list(range(1, chips, 2))[::-1]

    def hop(value, by):
        moves = [(ring[i], ring[(i + by) % chips]) for i in range(chips)]
        return lax.ppermute(value, "expert", [(2 * a + c, 2 * b + c) for a, b in moves for c in (0, 1)])

    def last_hop(value, by):
        moves = [(ring[i], ring[(i + by) % chips]) for i in range(chips)]
        return lax.ppermute(
            value,
            ("pipe", "expert"),
            [
                (s * experts + 2 * a + c, (s - 1) % sections * experts + 2 * b + c)
                for s in range(sections)
                for a, b in moves
                for c in (0, 1)
            ],
        )

    def to_previous(value):
        return lax.ppermute(value, "pipe", [(s, (s - 1) % sections) for s in range(sections)])

    def swap(value):
        return lax.ppermute(value, "expert", [(e, e ^ 1) for e in range(experts)])

    x, grad = bwd_input[0], out_grad[0]
    u0, d0 = up_weight[0, 0], down_weight[0, 0]
    e = lax.axis_index("expert").astype(jnp.int32)
    me = jnp.stack([e, e ^ 1])

    half = grad.shape[0] // 2
    u1, d1 = swap(u0), swap(d0)
    a, b, keep = pack(x, grad, norm_gain, bwd_routes[0], bwd_gates[0], experts)
    a1, b1 = hop(a, 1), hop(b, -1)
    weights = (*turn(u0, d0), *turn(u1, d1))
    own = expert_part(me, a, b, 2 * half, weights).astype(jnp.bfloat16)
    own_out, keep_out, grad_out = to_previous(own), to_previous(keep), to_previous(grad)
    early = {4: own, 2: keep_out, 3: grad_out, 6: own_out}
    sum_a = sum_b = None
    for step in range(1, chips):
        a, b = a1, b1
        if step in early:
            a, b, early[step] = lax.optimization_barrier((a, b, early[step]))
        if step < chips - 1:
            a1, b1 = hop(a, 1), hop(b, -1)
        part = expert_part(me, a, b, 2 * half, weights)
        part_a, part_b = part[:half], part[half:]
        if step > 1:
            part_a = part_a + sum_a.astype(jnp.float32)
            part_b = part_b + sum_b.astype(jnp.float32)
        send_a, send_b = part_a.astype(jnp.bfloat16), part_b.astype(jnp.bfloat16)
        move = hop if step < chips - 1 else last_hop
        sum_a, sum_b = move(send_a, 1), move(send_b, -1)
    held = settle(keep_out, grad_out, own_out)
    return finish(*held, sum_a, sum_b)[None]


def solution(mesh):
    return jax.shard_map(
        shards,
        mesh=mesh,
        in_specs=(
            P("pipe", "expert", None),
            P("pipe", "expert", None),
            P("pipe", None),
            P("pipe", "expert", None, None),
            P("pipe", "expert", None, None),
            P("pipe", "expert", None),
            P("pipe", "expert", None),
        ),
        out_specs=P("pipe", "expert", None),
        check_vma=False,
    )
```
